256 devices in a mesh: ctx: 32 (over y_hi, z, core), ch: 8 (over y_lo, x).
Axes of the slice: x: 4, y: 4 (y_hi: 2, y_lo: 2; y = y_hi * 2 + y_lo), z: 8, core: 2. Of those that a mesh axis runs over, the one named last changes fastest.
Arguments:
- streams: bfloat16 [16384, 3, 2048], P('ctx', None, 'ch'), may hold values from -6 to 6
- short_taps: float32 [3, 3, 2048], P(None, None, 'ch'), may hold values from -3 to 3
- filters: bfloat16 [16384, 2048], P('ctx', 'ch'), may hold values from -1 to 1, as said below
- skip_gain: float32 [2048], P('ch'), may hold values from 0.2 to 0.6
- out_weight: bfloat16 [2048, 4096], P('ch'), may hold values from -0.1875 to 0.1875
Outputs:
- output: bfloat16 [16384, 4096], P('ctx', 'ch')
The draws below stay inside these ranges and needn't reach their ends.
Inputs may be any that keep to these rules, and one draw needn't show every extreme that they name: `filters`: filter taps of every channel and lag.
All inputs are finite; a program needn't handle non-finite values.
Results may differ from the reference program's by a relative error of at most 0.017.
Values may be sent and summed in bfloat16 or wider, within the bound.
A program may use at most 128 MiB of HBM per device.

```python
import math
import jax
import jax.numpy as jnp
from jax import lax

D = 4096
CHAN = 2048
SEG = 512
TOKEN_LENGTH = 16384
N_CTX = 32
N_CH = 8


def draw_filters(key, part):
    base_key = jax.random.fold_in(key, 7)
    random_subkeys = jax.random.split(base_key, 6)
    delay_offsets = jnp.arange(TOKEN_LENGTH, dtype=jnp.float32)[:, None]
    random_noise = jnp.clip(jax.random.normal(random_subkeys[0], (TOKEN_LENGTH, CHAN), jnp.float32), -6.0, 6.0)
    fast_share = 0.25
    fast_mask = jax.random.uniform(random_subkeys[1], (1, CHAN), jnp.float32) < fast_share
    fast_rate = jnp.exp(jax.random.uniform(random_subkeys[2], (1, CHAN), jnp.float32, math.log(math.log(10.0) / 50.0), math.log(math.log(10.0) / 30.0)))
    slow_rate = jnp.exp(jax.random.uniform(random_subkeys[3], (1, CHAN), jnp.float32, math.log(0.02), math.log(0.2))) / TOKEN_LENGTH
    falloff_speed = jnp.where(fast_mask, fast_rate, slow_rate)
    signal_power = jnp.expm1(-2.0 * falloff_speed * TOKEN_LENGTH) / jnp.expm1(-2.0 * falloff_speed)
    spike_position = jax.random.randint(random_subkeys[4], (2,), 0, TOKEN_LENGTH)
    spike_retained = jax.random.uniform(random_subkeys[5], (2,), jnp.float32, 0.65, 0.8)
    spike_multiplier = jnp.ones((TOKEN_LENGTH, 1), jnp.float32)
    for index_vector in range(2):
        spike_multiplier = spike_multiplier * jnp.where(delay_offsets >= spike_position[index_vector].astype(jnp.float32), spike_retained[index_vector], 1.0)
    value_entries = random_noise * jnp.exp(-falloff_speed * delay_offsets) * spike_multiplier / jnp.sqrt(signal_power)
    return jnp.clip(value_entries, -1.0, 1.0).astype(jnp.bfloat16)


def with_spikes(entries, rng, source, target, blocks, factor):
    def block_of(position):
        return (jnp.arange(entries.shape[position]) // (entries.shape[position] // blocks)).reshape((-1,) + (1,) * (entries.ndim - 1 - position))

    one_side = jax.random.permutation(rng, blocks)[block_of(target)]
    far = (block_of(target) + blocks // 2) % blocks
    return jnp.where((block_of(source) == one_side) | (block_of(source) == far), factor * entries, entries)


def levels(rng, dims, pieces, low, high):
    gain = 1.0
    for position, shards_of in pieces:
        heights = jax.random.uniform(jax.random.fold_in(jax.random.fold_in(rng, 6), position), (shards_of,), jnp.float32, low / len(pieces), high / len(pieces))
        gain = gain * jnp.repeat(jnp.exp(heights), dims[position] // shards_of).reshape((-1,) + (1,) * (len(dims) - 1 - position))
    return gain


def scatter_about(rng, extent, scale, most, pieces=(), kind=jnp.bfloat16):
    loudness = levels(rng, extent, pieces, -0.22, 0.18) if pieces else 1.0
    drawn = jax.random.normal(rng, extent, jnp.float32) * scale * loudness
    return jnp.minimum(jnp.maximum(drawn, -most), most).astype(kind)


def heavy_noise(key, dims, scale, most, shards, heavy, kind=jnp.bfloat16):
    entries = scale * jax.random.normal(key, dims, jnp.float32)
    if shards:
        entries = entries * levels(key, dims, shards, -0.22, 0.18)
    return jnp.clip(with_spikes(entries, jax.random.fold_in(key, 3), *heavy), -most, most).astype(kind)


def setup_inputs(seed: int = 0) -> dict:
    key_of = jax.random.split(jax.random.key(seed), 6)
    return {
        "streams": scatter_about(key_of[0], (TOKEN_LENGTH, 3, CHAN), 1.0, 6.0, ((0, 32), (2, 8))),
        "short_taps": scatter_about(key_of[1], (3, 3, CHAN), 0.6, 3.0, ((2, 8),), jnp.float32),
        "filters": draw_filters(jax.random.fold_in(key_of[5], 71), 0),
        "skip_gain": jnp.clip(0.2 + 0.400000021 * jax.random.uniform(key_of[3], (CHAN,), jnp.float32) ** levels(key_of[3], (CHAN,), ((0, 8),), -0.2, 0.2), 0.2, 0.6),
        "out_weight": heavy_noise(key_of[4], (CHAN, D), CHAN ** -0.5, 0.1875, ((0, 8),), (0, 1, 8, 2.0)),
    }


def forward_table(size):
    half = size // 2
    rows = jnp.arange(size, dtype=jnp.int32)[:, None]
    cols = jnp.arange(size, dtype=jnp.int32)[None, :]
    freq = jnp.where(cols < half, cols, cols - half)
    phase = (rows * freq) % size
    angle = phase.astype(jnp.float32) * (2.0 * math.pi / size)
    cosine = jnp.cos(angle)
    sine = -jnp.sin(angle)
    nyquist = jnp.where(rows % 2 == 0, 1.0, -1.0).astype(jnp.float32)
    table = jnp.where(cols < half, cosine, jnp.where(cols == half, nyquist, sine))
    return table.astype(jnp.bfloat16)


def inverse_table(size):
    half = size // 2
    rows = jnp.arange(size, dtype=jnp.int32)[:, None]
    places = half + jnp.arange(half, dtype=jnp.int32)[None, :]
    freq = jnp.where(rows < half, rows, rows - half)
    phase = (places * freq) % size
    angle = phase.astype(jnp.float32) * (2.0 * math.pi / size)
    weight = jnp.where(freq == 0, 1.0, 2.0).astype(jnp.float32) / size
    cosine = weight * jnp.cos(angle)
    sine = -weight * jnp.sin(angle)
    nyquist = jnp.where(places % 2 == 0, 1.0, -1.0).astype(jnp.float32) / size
    table = jnp.where(rows < half, cosine, jnp.where(rows == half, nyquist, sine))
    return table.astype(jnp.bfloat16)


def spectrum_product(left, right):
    half = left.shape[-1] // 2
    right = right.astype(jnp.float32)
    left_re, left_im = left[..., :half], left[..., half:]
    right_re, right_im = right[..., :half], right[..., half:]
    inside = jnp.arange(half, dtype=jnp.int32) > 0
    real_part = left_re * right_re - jnp.where(inside, left_im * right_im, 0.0)
    imag_part = jnp.where(inside, left_re * right_im + left_im * right_re, left_im * right_im)
    return jnp.concatenate([real_part, imag_part], axis=-1)


def reference(streams, short_taps, filters, skip_gain, out_weight):
    seq_len = streams.shape[0]
    width = 2 * SEG
    padded = jnp.concatenate([jnp.zeros((2, 3, CHAN), streams.dtype), streams], axis=0)
    mixed = short_taps[0][None] * padded[2:].astype(jnp.float32)
    mixed = mixed + short_taps[1][None] * padded[1:seq_len + 1].astype(jnp.float32)
    mixed = mixed + short_taps[2][None] * padded[:seq_len].astype(jnp.float32)
    inner = (mixed[:, 0, :] * mixed[:, 1, :]).astype(jnp.bfloat16)
    forward = forward_table(width)
    backward = inverse_table(width)
    filt_blocks = filters.reshape(N_CTX, SEG, CHAN)
    earlier = jnp.concatenate([jnp.zeros((1, SEG, CHAN), filters.dtype), filt_blocks[:-1]], axis=0)
    windows = jnp.concatenate([earlier, filt_blocks], axis=1)
    filter_spectrum = jnp.einsum("nmc,mf->ncf", windows.astype(jnp.float32), forward.astype(jnp.float32)).astype(jnp.bfloat16)
    in_blocks = inner.reshape(N_CTX, SEG, CHAN)
    input_spectrum = jnp.einsum("nbc,bf->ncf", in_blocks.astype(jnp.float32), forward[:SEG].astype(jnp.float32))

    def one_block(target):
        def add_tile(source, total):
            return total + spectrum_product(input_spectrum[source], filter_spectrum[target - source])
        accumulated = lax.fori_loop(0, target + 1, add_tile, jnp.zeros((CHAN, width), jnp.float32))
        spectrum_low = accumulated.astype(jnp.bfloat16)
        return jnp.dot(spectrum_low, backward, preferred_element_type=jnp.float32).astype(jnp.bfloat16)

    long_blocks = lax.map(one_block, jnp.arange(N_CTX, dtype=jnp.int32))
    long_conv = jnp.transpose(long_blocks, (0, 2, 1)).reshape(seq_len, CHAN)
    gated = (mixed[:, 2, :] * (long_conv.astype(jnp.float32) + skip_gain[None, :] * inner.astype(jnp.float32))).astype(jnp.bfloat16)
    group = CHAN // N_CH
    summed = jnp.zeros((seq_len, D), jnp.float32)
    for index_vector in range(N_CH):
        partial_term = jnp.dot(gated[:, index_vector * group:(index_vector + 1) * group], out_weight[index_vector * group:(index_vector + 1) * group], preferred_element_type=jnp.float32)
        summed = summed + partial_term.astype(jnp.bfloat16).astype(jnp.float32)
    return summed.astype(jnp.bfloat16)
```

```python
import functools

import jax
import jax.numpy as jnp
import ml_dtypes
import numpy as np
from jax import lax
from jax.experimental import pallas as pl
from jax.experimental.pallas import tpu as pltpu
from jax.sharding import PartitionSpec as P

LANES = 128
GROUP = 4


def half_table(size):
    half = size // 2
    rows = np.arange(half, dtype=np.int64)[:, None]
    cols = np.arange(size, dtype=np.int64)[None, :]
    freq = np.where(cols < half, cols, cols - half)
    angle = (rows * freq % size).astype(np.float64) * (2.0 * np.pi / size)
    nyquist = np.where(rows % 2 == 0, 1.0, -1.0)
    table = np.where(cols < half, np.cos(angle), np.where(cols == half, nyquist, -np.sin(angle)))
    return table.astype(ml_dtypes.bfloat16)


def rows_of(ref):
    blocks, chans, width = ref.shape
    return ref[...].astype(jnp.float32).reshape(blocks * chans, width).astype(jnp.bfloat16)


def conv_kernel(x_ref, h_ref, f_ref, y_ref, xs, hs, low):
    blocks, chans, seg = x_ref.shape
    half = seg
    size = 2 * seg
    tiles = half // LANES
    lead = GROUP - 1
    table = f_ref[...]
    spec = jnp.dot(rows_of(x_ref), table, preferred_element_type=jnp.float32)
    for part in range(2):
        for q in range(tiles):
            at = part * half + q * LANES
            xs[part, q] = spec[:, at : at + LANES].reshape(blocks, chans, LANES)
    filt = jnp.dot(rows_of(h_ref), table, preferred_element_type=jnp.float32)
    lane = lax.broadcasted_iota(jnp.int32, (1, 1, LANES), 2)
    for q in range(tiles):
        inside = (lane > 0) if q == 0 else (lane >= 0)
        weight = jnp.where(inside, 2.0 / size, 1.0 / size).astype(jnp.float32)
        signed = jnp.where(lane % 2 == 0, weight, -weight)
        parts = []
        for part in range(2):
            at = part * half + q * LANES
            block = filt[:, at : at + LANES].reshape(blocks, chans, LANES)
            before = jnp.concatenate(
                [jnp.zeros((1, chans, LANES), jnp.float32), block[: blocks - 1]], axis=0
            )
            parts.append(before * signed + block * weight)
        real, imag = parts
        keep = jnp.broadcast_to(inside, real.shape)
        hs[0, q, lead:] = real
        hs[1, q, lead:] = jnp.where(keep, imag, 0.0)
        hs[2, q, lead:] = jnp.where(keep, real, imag)
        for kind in range(3):
            hs[kind, q, :lead] = jnp.zeros((lead, chans, LANES), jnp.float32)

    def one_tile(q, _):
        def one_group(big, _):
            def one_source(small, total):
                gap = big - small
                xr = [xs[0, q, GROUP * small + b] for b in range(GROUP)]
                xi = [xs[1, q, GROUP * small + b] for b in range(GROUP)]
                gr, gi, g2 = (
                    [hs[kind, q, GROUP * gap + m] for m in range(2 * GROUP - 1)]
                    for kind in range(3)
                )
                total = list(total)
                for a in range(GROUP):
                    for b in range(GROUP):
                        m = a - b + lead
                        total[a] += xr[b] * gr[m] - xi[b] * gi[m]
                        total[GROUP + a] += xr[b] * gi[m] + xi[b] * g2[m]
                return tuple(total)

            zero = jnp.zeros((chans, LANES), jnp.float32)
            total = lax.fori_loop(0, big + 1, one_source, (zero,) * (2 * GROUP))
            rows = pl.ds(pl.multiple_of(big * GROUP * chans, GROUP * chans), GROUP * chans)
            for part in range(2):
                cols = pl.ds(pl.multiple_of(part * half + q * LANES, LANES), LANES)
                piece = jnp.concatenate(total[part * GROUP : (part + 1) * GROUP], axis=0)
                low[rows, cols] = piece.astype(jnp.bfloat16)
            return 0

        return lax.fori_loop(0, blocks // GROUP, one_group, 0)

    lax.fori_loop(0, tiles, one_tile, 0)
    out = lax.dot_general(
        low[...], table, (((1,), (1,)), ((), ())), preferred_element_type=jnp.float32
    )
    y_ref[...] = out.reshape(blocks, chans, seg).astype(jnp.bfloat16)


def long_convolution(x, h, table):
    blocks, chans, seg = x.shape
    tiles = seg // LANES
    return pl.pallas_call(
        conv_kernel,
        out_shape=jax.ShapeDtypeStruct(x.shape, jnp.bfloat16),
        in_specs=[pl.BlockSpec(memory_space=pltpu.VMEM)] * 3,
        out_specs=pl.BlockSpec(memory_space=pltpu.VMEM),
        scratch_shapes=[
            pltpu.VMEM((2, tiles, blocks, chans, LANES), jnp.float32),
            pltpu.VMEM((3, tiles, blocks + GROUP - 1, chans, LANES), jnp.float32),
            pltpu.VMEM((blocks * chans, 2 * seg), jnp.bfloat16),
        ],
        compiler_params=pltpu.CompilerParams(vmem_limit_bytes=32 << 20),
        name="long_convolution",
    )(x, h, table)


def passed_along(value, axis, steps):
    count = lax.axis_size(axis)
    initial, last = (max(0, -steps), min(count, count - steps))
    return lax.ppermute(value, axis, [(source, source + steps) for source in range(initial, last)])


def local(streams, short_taps, filters, skip_gain, out_weight, *, table):
    block_rows = streams.shape[0]
    channels = streams.shape[2]
    count = lax.axis_size("ctx")
    share = channels // count
    edge_rows = passed_along(streams[block_rows - 2 :], "ctx", 1)
    extended = jnp.concatenate([edge_rows, streams], axis=0)
    mixed = short_taps[0][None] * extended[2:].astype(jnp.float32)
    mixed = mixed + short_taps[1][None] * extended[1 : block_rows + 1].astype(jnp.float32)
    mixed = mixed + short_taps[2][None] * extended[:block_rows].astype(jnp.float32)
    inner = (mixed[:, 0, :] * mixed[:, 1, :]).astype(jnp.bfloat16)
    both = jnp.stack([inner.T, filters.T]).reshape(2, count, share, block_rows)
    both = lax.all_to_all(both, "ctx", 1, 1, tiled=True)
    mine = long_convolution(both[0], both[1], table)
    back = lax.all_to_all(mine, "ctx", 0, 0, tiled=True)
    long_conv = back.reshape(channels, block_rows).T
    gated = (
        mixed[:, 2, :]
        * (long_conv.astype(jnp.float32) + skip_gain[None, :] * inner.astype(jnp.float32))
    ).astype(jnp.bfloat16)
    weight = lax.all_to_all(out_weight, "ch", 1, 0, tiled=True)
    every = lax.all_gather(gated, "ch", axis=1, tiled=True)
    return jnp.dot(every, weight, preferred_element_type=jnp.float32).astype(jnp.bfloat16)


def solution(mesh):
    seg = 16384 // mesh.shape["ctx"]
    table = half_table(2 * seg)
    return jax.shard_map(
        functools.partial(local, table=table),
        mesh=mesh,
        in_specs=(
            P("ctx", None, "ch"),
            P(None, None, "ch"),
            P("ctx", "ch"),
            P("ch"),
            P("ch", None),
        ),
        out_specs=P("ctx", "ch"),
        check_vma=False,
    )
```

```python
import functools

import jax
import jax.numpy as jnp
import ml_dtypes
import numpy as np
from jax import lax
from jax.experimental import pallas as pl
from jax.experimental.pallas import tpu as pltpu
from jax.sharding import PartitionSpec as P

LANES = 128
GROUP = 4
CHUNKS = 2
RING = 4
EDGE = 16
MESH = pl.DeviceIdType.MESH
F32 = jnp.float32
BF16 = jnp.bfloat16


def half_table(size):
    half = size // 2
    rows = np.arange(half, dtype=np.int64)[:, None]
    cols = np.arange(size, dtype=np.int64)[None, :]
    freq = np.where(cols < half, cols, cols - half)
    angle = (rows * freq % size).astype(np.float64) * (2.0 * np.pi / size)
    nyquist = np.where(rows % 2 == 0, 1.0, -1.0)
    table = np.where(cols < half, np.cos(angle), np.where(cols == half, nyquist, -np.sin(angle)))
    return table.astype(ml_dtypes.bfloat16)


def rows_of(ref):
    blocks, chans, width = ref.shape
    return ref[...].astype(F32).reshape(blocks * chans, width).astype(BF16)


def source_spectra(x_ref, table, xs):
    blocks, chans, half = x_ref.shape
    spec = jnp.dot(rows_of(x_ref), table[...], preferred_element_type=F32)
    for part in range(2):
        for q in range(half // LANES):
            at = part * half + q * LANES
            xs[part, q] = spec[:, at : at + LANES].reshape(blocks, chans, LANES)


def filter_spectra(h_ref, table, hs):
    blocks, chans, half = h_ref.shape
    size = 2 * half
    lead = GROUP - 1
    filt = jnp.dot(rows_of(h_ref), table[...], preferred_element_type=F32)
    lane = lax.broadcasted_iota(jnp.int32, (1, 1, LANES), 2)
    for q in range(half // LANES):
        inside = (lane > 0) if q == 0 else (lane >= 0)
        weight = jnp.where(inside, 2.0 / size, 1.0 / size).astype(F32)
        signed = jnp.where(lane % 2 == 0, weight, -weight)
        parts = []
        for part in range(2):
            at = part * half + q * LANES
            block = filt[:, at : at + LANES].reshape(blocks, chans, LANES)
            before = jnp.concatenate(
                [jnp.zeros((1, chans, LANES), F32), block[: blocks - 1]], axis=0
            )
            parts.append(before * signed + block * weight)
        real, imag = parts
        keep = jnp.broadcast_to(inside, real.shape)
        hs[0, q, lead:] = real
        hs[1, q, lead:] = jnp.where(keep, imag, 0.0)
        hs[2, q, lead:] = jnp.where(keep, real, imag)
        for kind in range(3):
            hs[kind, q, :lead] = jnp.zeros((lead, chans, LANES), F32)


def block_products(xs, hs, low):
    _, tiles, blocks, chans, _ = xs.shape
    half = tiles * LANES
    lead = GROUP - 1

    def one_tile(q, _):
        def one_group(big, _):
            def one_source(small, total):
                gap = big - small
                xr = [xs[0, q, GROUP * small + b] for b in range(GROUP)]
                xi = [xs[1, q, GROUP * small + b] for b in range(GROUP)]
                gr, gi, g2 = (
                    [hs[kind, q, GROUP * gap + m] for m in range(2 * GROUP - 1)]
                    for kind in range(3)
                )
                total = list(total)
                for a in range(GROUP):
                    for b in range(GROUP):
                        m = a - b + lead
                        total[a] += xr[b] * gr[m] - xi[b] * gi[m]
                        total[GROUP + a] += xr[b] * gi[m] + xi[b] * g2[m]
                return tuple(total)

            zero = jnp.zeros((chans, LANES), F32)
            total = lax.fori_loop(0, big + 1, one_source, (zero,) * (2 * GROUP))
            rows = pl.ds(pl.multiple_of(big * GROUP * chans, GROUP * chans), GROUP * chans)
            for part in range(2):
                cols = pl.ds(pl.multiple_of(part * half + q * LANES, LANES), LANES)
                piece = jnp.concatenate(total[part * GROUP : (part + 1) * GROUP], axis=0)
                low[rows, cols] = piece.astype(BF16)
            return 0

        return lax.fori_loop(0, blocks // GROUP, one_group, 0)

    lax.fori_loop(0, tiles, one_tile, 0)


def take(sem, ref):
    pltpu.make_async_copy(ref, ref, sem).wait()


def operator_kernel(
    n_ctx,
    n_ch,
    streams,
    taps_in,
    filters,
    skip_in,
    table_in,
    weight,
    out,
    strm,
    taps,
    filt,
    skip,
    table,
    wide,
    pad,
    halo,
    send_h,
    recv_h,
    send_x,
    recv_x,
    send_y,
    recv_y,
    xs,
    hs,
    low,
    outer,
    direct,
    gat,
    acc,
    out_v,
    local_sem,
    halo_sem,
    h_sem,
    x_sem,
    y_sem,
    w_sem,
    f_sem,
    g_send,
    g_recv,
    out_sem,
):
    me = lax.axis_index("ctx")
    col = lax.axis_index("ch")
    core = lax.rem(me, 2)
    partner = me + 1 - 2 * core
    _, seg, chans = streams.shape
    share = chans // n_ctx
    cols = weight.shape[1] // n_ch
    rows = chans // 2
    step = seg // CHUNKS

    own_cols = pl.ds(pl.multiple_of(col * cols, cols), cols)
    loads = [
        pltpu.make_async_copy(filters, filt, local_sem.at[0]),
        pltpu.make_async_copy(streams, strm, local_sem.at[1]),
        pltpu.make_async_copy(taps_in, taps, local_sem.at[2]),
        pltpu.make_async_copy(skip_in, skip, local_sem.at[3]),
        pltpu.make_async_copy(table_in, table, local_sem.at[4]),
        pltpu.make_async_copy(weight.at[:, own_cols], wide.at[col], local_sem.at[5]),
    ]
    for load in loads:
        load.start()

    barrier = pltpu.get_barrier_semaphore()

    def greet_ctx(k, _):
        pl.semaphore_signal(
            barrier, inc=1, device_id={"ctx": lax.rem(me + k, n_ctx)}, device_id_type=MESH
        )
        return 0

    def greet_ch(k, _):
        pl.semaphore_signal(
            barrier, inc=1, device_id={"ch": lax.rem(col + k, n_ch)}, device_id_type=MESH
        )
        return 0

    lax.fori_loop(1, n_ctx, greet_ctx, 0)
    lax.fori_loop(1, n_ch, greet_ch, 0)

    loads[0].wait()
    send_h[...] = filt[...].astype(F32).T.reshape(n_ctx, share, seg).astype(BF16)
    recv_h[me] = send_h[me]
    pl.semaphore_wait(barrier, n_ctx - 1 + n_ch - 1)

    edge = pltpu.make_async_remote_copy(
        src_ref=streams.at[:, pl.ds(seg - EDGE, EDGE), :],
        dst_ref=halo,
        send_sem=halo_sem.at[0],
        recv_sem=halo_sem.at[1],
        device_id={"ctx": lax.rem(me + 1, n_ctx)},
        device_id_type=MESH,
    )
    edge.start()

    def exchange(source, target, sem):
        def one(k, _):
            reach = lax.div(k + 1, 2)
            there = lax.rem(me + jnp.where(lax.rem(k, 2) == 1, reach, n_ctx - reach), n_ctx)
            pltpu.make_async_remote_copy(
                src_ref=source.at[there],
                dst_ref=target.at[me],
                send_sem=sem.at[0],
                recv_sem=sem.at[1],
                device_id={"ctx": there},
                device_id_type=MESH,
            ).start()
            return 0

        lax.fori_loop(1, n_ctx, one, 0)

    exchange(send_h, recv_h, h_sem)

    loads[1].wait()
    loads[2].wait()
    loads[3].wait()
    for q in range(3):
        pad[q, 8:] = strm[q].astype(F32)
    edge.wait_recv()
    pad[:, :8] = jnp.where(me > 0, halo[...].astype(F32)[:, EDGE - 8 :], 0.0)
    piece = min(LANES, seg)
    for at in range(0, seg, piece):

        def mixed(q):
            total = taps[0, q : q + 1] * pad[q, 8 + at : 8 + at + piece]
            total = total + taps[1, q : q + 1] * pad[q, 7 + at : 7 + at + piece]
            return total + taps[2, q : q + 1] * pad[q, 6 + at : 6 + at + piece]

        inner = (mixed(0) * mixed(1)).astype(BF16).astype(F32)
        send_x[:, :, at : at + piece] = inner.T.reshape(n_ctx, share, piece).astype(BF16)
        direct[at : at + piece] = skip[...] * inner
        outer[at : at + piece] = mixed(2)
    recv_x[me] = send_x[me]
    exchange(send_x, recv_x, x_sem)

    half_rows = pl.ds(pl.multiple_of(core * rows, rows), rows)

    def lend(k, _):
        there = lax.rem(col + k, n_ch)
        pltpu.make_async_remote_copy(
            src_ref=weight.at[half_rows, pl.ds(pl.multiple_of(there * cols, cols), cols)],
            dst_ref=wide.at[col, half_rows],
            send_sem=w_sem.at[0],
            recv_sem=w_sem.at[1],
            device_id={"ch": there},
            device_id_type=MESH,
        ).start()
        return 0

    lax.fori_loop(1, n_ch, lend, 0)

    loads[4].wait()
    others = pl.ds(0, n_ctx - 1)
    take(h_sem.at[1], recv_h.at[others])
    filter_spectra(recv_h, table, hs)
    take(x_sem.at[1], recv_x.at[others])
    source_spectra(recv_x, table, xs)
    block_products(xs, hs, low)
    for kk in range(CHUNKS):
        part = lax.dot_general(
            low[...],
            table[kk * step : (kk + 1) * step],
            (((1,), (1,)), ((), ())),
            preferred_element_type=F32,
        )
        send_y[kk] = part.reshape(n_ctx, share, step).astype(BF16)
        recv_y[kk, me] = send_y[kk, me]
        exchange(send_y.at[kk], recv_y.at[kk], y_sem.at[kk])

    base = RING * lax.div(col, RING)
    place = lax.rem(col, RING)
    right = base + lax.rem(place + 1, RING)
    left = base + lax.rem(place + RING - 1, RING)
    far = base + lax.rem(place + 2, RING)
    swap = RING - 2 * base
    across, a_left, a_right, a_far = (c + swap for c in (col, left, right, far))
    full, first, second = pl.ds(0, step), pl.ds(0, step // 2), pl.ds(step // 2, step // 2)

    def hop(kk, kind, block, span, there):
        return pltpu.make_async_remote_copy(
            src_ref=gat.at[block, kk, span],
            dst_ref=gat.at[block, kk, span],
            send_sem=g_send.at[kk, kind],
            recv_sem=g_recv.at[kk, kind],
            device_id={"ch": there},
            device_id_type=MESH,
        )

    sent = []

    def push(*what):
        copy = hop(*what)
        copy.start()
        sent.append(copy)

    def arrived(kk, kind, block, span):
        hop(kk, kind, block, span, across).wait_recv()

    forward = []
    for kk in range(CHUNKS):
        take(y_sem.at[kk, 1], recv_y.at[kk, others])
        conv = recv_y[kk].astype(F32).reshape(chans, step).T
        at = kk * step
        gated = outer[at : at + step] * (conv + direct[at : at + step])
        gat[col, kk] = gated.astype(BF16)
        push(kk, 0, col, full, right)
        push(kk, 1, col, full, left)
        push(kk, 2, col, full, across)
    take(w_sem.at[1], wide.at[pl.ds(0, n_ch - 1), pl.ds(0, rows)])

    def pass_on(k, _):
        block = lax.rem(col + k, n_ch)
        pltpu.make_async_remote_copy(
            src_ref=wide.at[block, half_rows],
            dst_ref=wide.at[block, half_rows],
            send_sem=f_sem.at[0],
            recv_sem=f_sem.at[1],
            device_id={"ctx": partner},
            device_id_type=MESH,
        ).start()
        return 0

    lax.fori_loop(1, n_ch, pass_on, 0)

    for kk in range(CHUNKS):
        arrived(kk, 0, left, full)
        push(kk, 3, left, first, right)
        arrived(kk, 1, right, full)
        push(kk, 4, right, second, left)
        arrived(kk, 2, across, full)
        push(kk, 5, across, full, right)
        push(kk, 6, across, full, left)
    for kk in range(CHUNKS):
        arrived(kk, 3, far, first)
        arrived(kk, 4, far, second)
        push(kk, 7, far, full, across)
    loads[5].wait()
    take(f_sem.at[1], wide.at[pl.ds(0, n_ch - 1), pl.ds(0, rows)])

    def product(block, kk):
        return jnp.dot(gat[block, kk], wide[block], preferred_element_type=F32)

    for kk in range(CHUNKS):
        near = product(col, kk) + product(left, kk)
        acc[kk] = near + (product(right, kk) + product(across, kk)) + product(far, kk)
    for kk in range(CHUNKS):
        arrived(kk, 5, a_left, full)
        arrived(kk, 6, a_right, full)
        acc[kk] += product(a_left, kk) + product(a_right, kk)
    stores = []
    for kk in range(CHUNKS):
        arrived(kk, 7, a_far, full)
        span = pl.ds(kk * step, step)
        out_v[span] = (acc[kk] + product(a_far, kk)).astype(BF16)
        stores.append(pltpu.make_async_copy(out_v.at[span], out.at[span], out_sem.at[kk]))
        stores[-1].start()

    edge.wait_send()
    take(h_sem.at[0], send_h.at[others])
    take(x_sem.at[0], send_x.at[others])
    for kk in range(CHUNKS):
        take(y_sem.at[kk, 0], send_y.at[kk, others])
    take(w_sem.at[0], wide.at[pl.ds(0, n_ch - 1), pl.ds(0, rows)])
    take(f_sem.at[0], wide.at[pl.ds(0, n_ch - 1), pl.ds(0, rows)])
    for copy in sent:
        copy.wait_send()
    for store in stores:
        store.wait()


def local(streams, short_taps, filters, skip_gain, out_weight, *, table):
    n_ctx, n_ch = lax.axis_size("ctx"), lax.axis_size("ch")
    seg, _, chans = streams.shape
    share = chans // n_ctx
    cols = out_weight.shape[1] // n_ch
    tiles = seg // LANES
    step = seg // CHUNKS
    slabs = pltpu.VMEM((n_ctx, share, seg), BF16)
    pieces = pltpu.VMEM((CHUNKS, n_ctx, share, step), BF16)
    dma = pltpu.SemaphoreType.DMA
    return pl.pallas_call(
        functools.partial(operator_kernel, n_ctx, n_ch),
        out_shape=jax.ShapeDtypeStruct((seg, cols), BF16),
        in_specs=[pl.BlockSpec(memory_space=pl.ANY)] * 6,
        out_specs=pl.BlockSpec(memory_space=pl.ANY),
        scratch_shapes=[
            pltpu.VMEM((3, seg, chans), BF16),
            pltpu.VMEM(short_taps.shape, F32),
            pltpu.VMEM((seg, chans), BF16),
            pltpu.VMEM((1, chans), F32),
            pltpu.VMEM((seg, 2 * seg), BF16),
            pltpu.VMEM((n_ch, chans, cols), BF16),
            pltpu.VMEM((3, seg + 8, chans), F32),
            pltpu.VMEM((3, EDGE, chans), BF16),
            slabs,
            slabs,
            slabs,
            slabs,
            pieces,
            pieces,
            pltpu.VMEM((2, tiles, n_ctx, share, LANES), F32),
            pltpu.VMEM((3, tiles, n_ctx + GROUP - 1, share, LANES), F32),
            pltpu.VMEM((n_ctx * share, 2 * seg), BF16),
            pltpu.VMEM((seg, chans), F32),
            pltpu.VMEM((seg, chans), F32),
            pltpu.VMEM((n_ch, CHUNKS, step, chans), BF16),
            pltpu.VMEM((CHUNKS, step, cols), F32),
            pltpu.VMEM((seg, cols), BF16),
            dma((6,)),
            dma((2,)),
            dma((2,)),
            dma((2,)),
            dma((CHUNKS, 2)),
            dma((2,)),
            dma((2,)),
            dma((CHUNKS, 8)),
            dma((CHUNKS, 8)),
            dma((CHUNKS,)),
        ],
        compiler_params=pltpu.CompilerParams(
            collective_id=0, has_side_effects=True, vmem_limit_bytes=48 << 20
        ),
        name="hyena_operator",
    )(
        jnp.transpose(streams, (1, 0, 2)),
        short_taps,
        filters,
        skip_gain[None],
        table,
        out_weight,
    )


def solution(mesh):
    seg = 16384 // mesh.shape["ctx"]
    return jax.shard_map(
        functools.partial(local, table=half_table(2 * seg)),
        mesh=mesh,
        in_specs=(
            P("ctx", None, "ch"),
            P(None, None, "ch"),
            P("ctx", "ch"),
            P("ch"),
            P("ch", None),
        ),
        out_specs=P("ctx", "ch"),
        check_vma=False,
    )
```

```python
import functools

import jax
import jax.numpy as jnp
import ml_dtypes
import numpy as np
from jax import lax
from jax.experimental import pallas as pl
from jax.experimental.pallas import tpu as pltpu
from jax.sharding import PartitionSpec as P

LANES = 128
GROUP = 4
CHUNKS = 2
RING = 4
EDGE = 16
MESH = pl.DeviceIdType.MESH
F32 = jnp.float32
BF16 = jnp.bfloat16


def half_table(size):
    half = size // 2
    rows = np.arange(half, dtype=np.int64)[:, None]
    cols = np.arange(size, dtype=np.int64)[None, :]
    freq = np.where(cols < half, cols, cols - half)
    angle = (rows * freq % size).astype(np.float64) * (2.0 * np.pi / size)
    nyquist = np.where(rows % 2 == 0, 1.0, -1.0)
    table = np.where(cols < half, np.cos(angle), np.where(cols == half, nyquist, -np.sin(angle)))
    return table.astype(ml_dtypes.bfloat16)


def rows_of(ref):
    blocks, chans, width = ref.shape
    return ref[...].astype(F32).reshape(blocks * chans, width).astype(BF16)


def source_spectra(x_ref, table, xs):
    blocks, chans, half = x_ref.shape
    spec = jnp.dot(rows_of(x_ref), table[...], preferred_element_type=F32)
    for part in range(2):
        for q in range(half // LANES):
            at = part * half + q * LANES
            xs[part, q] = spec[:, at : at + LANES].reshape(blocks, chans, LANES)


def filter_spectra(h_ref, table, hs):
    blocks, chans, half = h_ref.shape
    size = 2 * half
    lead = GROUP - 1
    filt = jnp.dot(rows_of(h_ref), table[...], preferred_element_type=F32)
    lane = lax.broadcasted_iota(jnp.int32, (1, 1, LANES), 2)
    for q in range(half // LANES):
        inside = (lane > 0) if q == 0 else (lane >= 0)
        weight = jnp.where(inside, 2.0 / size, 1.0 / size).astype(F32)
        signed = jnp.where(lane % 2 == 0, weight, -weight)
        parts = []
        for part in range(2):
            at = part * half + q * LANES
            block = filt[:, at : at + LANES].reshape(blocks, chans, LANES)
            before = jnp.concatenate(
                [jnp.zeros((1, chans, LANES), F32), block[: blocks - 1]], axis=0
            )
            parts.append(before * signed + block * weight)
        real, imag = parts
        keep = jnp.broadcast_to(inside, real.shape)
        hs[0, q, lead:] = real
        hs[1, q, lead:] = jnp.where(keep, imag, 0.0)
        hs[2, q, lead:] = jnp.where(keep, real, imag)
        for kind in range(3):
            hs[kind, q, :lead] = jnp.zeros((lead, chans, LANES), F32)


def block_products(xs, hs, low):
    _, tiles, blocks, chans, _ = xs.shape
    half = tiles * LANES
    lead = GROUP - 1

    def one_tile(q, _):
        def one_group(big, _):
            def one_source(small, total):
                gap = big - small
                xr = [xs[0, q, GROUP * small + b] for b in range(GROUP)]
                xi = [xs[1, q, GROUP * small + b] for b in range(GROUP)]
                gr, gi, g2 = (
                    [hs[kind, q, GROUP * gap + m] for m in range(2 * GROUP - 1)]
                    for kind in range(3)
                )
                total = list(total)
                for a in range(GROUP):
                    for b in range(GROUP):
                        m = a - b + lead
                        total[a] += xr[b] * gr[m] - xi[b] * gi[m]
                        total[GROUP + a] += xr[b] * gi[m] + xi[b] * g2[m]
                return tuple(total)

            zero = jnp.zeros((chans, LANES), F32)
            total = lax.fori_loop(0, big + 1, one_source, (zero,) * (2 * GROUP))
            rows = pl.ds(pl.multiple_of(big * GROUP * chans, GROUP * chans), GROUP * chans)
            for part in range(2):
                cols = pl.ds(pl.multiple_of(part * half + q * LANES, LANES), LANES)
                piece = jnp.concatenate(total[part * GROUP : (part + 1) * GROUP], axis=0)
                low[rows, cols] = piece.astype(BF16)
            return 0

        return lax.fori_loop(0, blocks // GROUP, one_group, 0)

    lax.fori_loop(0, tiles, one_tile, 0)


def take(sem, ref):
    pltpu.make_async_copy(ref, ref, sem).wait()


def operator_kernel(
    n_ctx,
    n_ch,
    streams,
    taps_in,
    filters,
    skip_in,
    table_in,
    weight,
    out,
    strm,
    taps,
    filt,
    skip,
    table,
    wide,
    pad,
    halo,
    send_h,
    recv_h,
    send_x,
    recv_x,
    send_y,
    recv_y,
    xs,
    hs,
    low,
    outer,
    direct,
    gat,
    acc,
    out_v,
    local_sem,
    halo_sem,
    h_sem,
    x_sem,
    y_sem,
    w_sem,
    f_sem,
    g_send,
    g_recv,
    out_sem,
):
    me = lax.axis_index("ctx")
    col = lax.axis_index("ch")
    core = lax.rem(me, 2)
    partner = me + 1 - 2 * core
    _, seg, chans = streams.shape
    share = chans // n_ctx
    cols = weight.shape[1] // n_ch
    rows = chans // 2
    step = seg // CHUNKS

    own_cols = pl.ds(pl.multiple_of(col * cols, cols), cols)
    loads = [
        pltpu.make_async_copy(filters, filt, local_sem.at[0]),
        pltpu.make_async_copy(streams, strm, local_sem.at[1]),
        pltpu.make_async_copy(taps_in, taps, local_sem.at[2]),
        pltpu.make_async_copy(skip_in, skip, local_sem.at[3]),
        pltpu.make_async_copy(table_in, table, local_sem.at[4]),
        pltpu.make_async_copy(weight.at[:, own_cols], wide.at[col], local_sem.at[5]),
    ]
    for load in loads:
        load.start()

    barrier = pltpu.get_barrier_semaphore()

    def greet_ctx(k, _):
        pl.semaphore_signal(
            barrier, inc=1, device_id={"ctx": lax.rem(me + k, n_ctx)}, device_id_type=MESH
        )
        return 0

    def greet_ch(k, _):
        pl.semaphore_signal(
            barrier, inc=1, device_id={"ch": lax.rem(col + k, n_ch)}, device_id_type=MESH
        )
        return 0

    lax.fori_loop(1, n_ctx, greet_ctx, 0)
    lax.fori_loop(1, n_ch, greet_ch, 0)

    loads[0].wait()
    send_h[...] = filt[...].astype(F32).T.reshape(n_ctx, share, seg).astype(BF16)
    recv_h[me] = send_h[me]
    pl.semaphore_wait(barrier, n_ctx - 1 + n_ch - 1)

    edge = pltpu.make_async_remote_copy(
        src_ref=streams.at[:, pl.ds(seg - EDGE, EDGE), :],
        dst_ref=halo,
        send_sem=halo_sem.at[0],
        recv_sem=halo_sem.at[1],
        device_id={"ctx": lax.rem(me + 1, n_ctx)},
        device_id_type=MESH,
    )
    edge.start()

    def exchange(source, target, sem):
        def one(k, _):
            reach = lax.div(k + 1, 2)
            there = lax.rem(me + jnp.where(lax.rem(k, 2) == 1, reach, n_ctx - reach), n_ctx)
            pltpu.make_async_remote_copy(
                src_ref=source.at[there],
                dst_ref=target.at[me],
                send_sem=sem.at[0],
                recv_sem=sem.at[1],
                device_id={"ctx": there},
                device_id_type=MESH,
            ).start()
            return 0

        lax.fori_loop(1, n_ctx, one, 0)

    exchange(send_h, recv_h, h_sem)

    loads[1].wait()
    loads[2].wait()
    loads[3].wait()
    for q in range(3):
        pad[q, 8:] = strm[q].astype(F32)
    edge.wait_recv()
    pad[:, :8] = jnp.where(me > 0, halo[...].astype(F32)[:, EDGE - 8 :], 0.0)
    piece = min(LANES, seg)
    for at in range(0, seg, piece):

        def mixed(q):
            total = taps[0, q : q + 1] * pad[q, 8 + at : 8 + at + piece]
            total = total + taps[1, q : q + 1] * pad[q, 7 + at : 7 + at + piece]
            return total + taps[2, q : q + 1] * pad[q, 6 + at : 6 + at + piece]

        inner = (mixed(0) * mixed(1)).astype(BF16).astype(F32)
        send_x[:, :, at : at + piece] = inner.T.reshape(n_ctx, share, piece).astype(BF16)
        direct[at : at + piece] = skip[...] * inner
        outer[at : at + piece] = mixed(2)
    recv_x[me] = send_x[me]
    exchange(send_x, recv_x, x_sem)

    half_rows = pl.ds(pl.multiple_of(core * rows, rows), rows)

    def lend(k, _):
        there = lax.rem(col + k, n_ch)
        pltpu.make_async_remote_copy(
            src_ref=weight.at[half_rows, pl.ds(pl.multiple_of(there * cols, cols), cols)],
            dst_ref=wide.at[col, half_rows],
            send_sem=w_sem.at[0],
            recv_sem=w_sem.at[1],
            device_id={"ch": there},
            device_id_type=MESH,
        ).start()
        return 0

    lax.fori_loop(1, n_ch, lend, 0)

    loads[4].wait()
    others = pl.ds(0, n_ctx - 1)
    take(h_sem.at[1], recv_h.at[others])
    filter_spectra(recv_h, table, hs)
    take(x_sem.at[1], recv_x.at[others])
    source_spectra(recv_x, table, xs)
    block_products(xs, hs, low)
    for kk in range(CHUNKS):
        part = lax.dot_general(
            low[...],
            table[kk * step : (kk + 1) * step],
            (((1,), (1,)), ((), ())),
            preferred_element_type=F32,
        )
        send_y[kk] = part.reshape(n_ctx, share, step).astype(BF16)
        recv_y[kk, me] = send_y[kk, me]
        exchange(send_y.at[kk], recv_y.at[kk], y_sem.at[kk])

    base = RING * lax.div(col, RING)
    place = lax.rem(col, RING)
    right = base + lax.rem(place + 1, RING)
    left = base + lax.rem(place + RING - 1, RING)
    far = base + lax.rem(place + 2, RING)
    swap = RING - 2 * base
    across, a_left, a_right, a_far = (c + swap for c in (col, left, right, far))
    full, first, second = pl.ds(0, step), pl.ds(0, step // 2), pl.ds(step // 2, step // 2)

    def hop(kk, kind, block, span, there):
        return pltpu.make_async_remote_copy(
            src_ref=gat.at[block, kk, span],
            dst_ref=gat.at[block, kk, span],
            send_sem=g_send.at[kk, kind],
            recv_sem=g_recv.at[kk, kind],
            device_id={"ch": there},
            device_id_type=MESH,
        )

    sent = []

    def push(*what):
        copy = hop(*what)
        copy.start()
        sent.append(copy)

    def arrived(kk, kind, block, span):
        hop(kk, kind, block, span, across).wait_recv()

    forward = []
    for kk in range(CHUNKS):
        take(y_sem.at[kk, 1], recv_y.at[kk, others])
        conv = recv_y[kk].astype(F32).reshape(chans, step).T
        at = kk * step
        gated = outer[at : at + step] * (conv + direct[at : at + step])
        gat[col, kk] = gated.astype(BF16)
        push(kk, 0, col, full, right)
        push(kk, 1, col, full, left)
        push(kk, 2, col, full, across)
    take(w_sem.at[1], wide.at[pl.ds(0, n_ch - 1), pl.ds(0, rows)])

    def pass_on(k, _):
        block = lax.rem(col + k, n_ch)
        pltpu.make_async_remote_copy(
            src_ref=wide.at[block, half_rows],
            dst_ref=wide.at[block, half_rows],
            send_sem=f_sem.at[0],
            recv_sem=f_sem.at[1],
            device_id={"ctx": partner},
            device_id_type=MESH,
        ).start()
        return 0

    lax.fori_loop(1, n_ch, pass_on, 0)

    for kk in range(CHUNKS):
        arrived(kk, 0, left, full)
        push(kk, 3, left, first, right)
        arrived(kk, 1, right, full)
        push(kk, 4, right, second, left)
        arrived(kk, 2, across, full)
        push(kk, 5, across, full, right)
        push(kk, 6, across, full, left)
    for kk in range(CHUNKS):
        arrived(kk, 3, far, first)
        arrived(kk, 4, far, second)
        push(kk, 7, far, full, across)
    loads[5].wait()
    take(f_sem.at[1], wide.at[pl.ds(0, n_ch - 1), pl.ds(0, rows)])

    def product(block, kk):
        return jnp.dot(gat[block, kk], wide[block], preferred_element_type=F32)

    for kk in range(CHUNKS):
        near = product(col, kk) + product(left, kk)
        acc[kk] = near + (product(right, kk) + product(across, kk)) + product(far, kk)
    for kk in range(CHUNKS):
        arrived(kk, 5, a_left, full)
        arrived(kk, 6, a_right, full)
        acc[kk] += product(a_left, kk) + product(a_right, kk)
    stores = []
    for kk in range(CHUNKS):
        arrived(kk, 7, a_far, full)
        span = pl.ds(kk * step, step)
        out_v[span] = (acc[kk] + product(a_far, kk)).astype(BF16)
        stores.append(pltpu.make_async_copy(out_v.at[span], out.at[span], out_sem.at[kk]))
        stores[-1].start()

    edge.wait_send()
    take(h_sem.at[0], send_h.at[others])
    take(x_sem.at[0], send_x.at[others])
    for kk in range(CHUNKS):
        take(y_sem.at[kk, 0], send_y.at[kk, others])
    take(w_sem.at[0], wide.at[pl.ds(0, n_ch - 1), pl.ds(0, rows)])
    take(f_sem.at[0], wide.at[pl.ds(0, n_ch - 1), pl.ds(0, rows)])
    for copy in sent:
        copy.wait_send()
    for store in stores:
        store.wait()


def local(streams, short_taps, filters, skip_gain, out_weight, *, table):
    n_ctx, n_ch = lax.axis_size("ctx"), lax.axis_size("ch")
    seg, _, chans = streams.shape
    share = chans // n_ctx
    cols = out_weight.shape[1] // n_ch
    tiles = seg // LANES
    step = seg // CHUNKS
    slabs = pltpu.VMEM((n_ctx, share, seg), BF16)
    pieces = pltpu.VMEM((CHUNKS, n_ctx, share, step), BF16)
    dma = pltpu.SemaphoreType.DMA
    return pl.pallas_call(
        functools.partial(operator_kernel, n_ctx, n_ch),
        out_shape=jax.ShapeDtypeStruct((seg, cols), BF16),
        in_specs=[pl.BlockSpec(memory_space=pl.ANY)] * 6,
        out_specs=pl.BlockSpec(memory_space=pl.ANY),
        scratch_shapes=[
            pltpu.VMEM((3, seg, chans), BF16),
            pltpu.VMEM(short_taps.shape, F32),
            pltpu.VMEM((seg, chans), BF16),
            pltpu.VMEM((1, chans), F32),
            pltpu.VMEM((seg, 2 * seg), BF16),
            pltpu.VMEM((n_ch, chans, cols), BF16),
            pltpu.VMEM((3, seg + 8, chans), F32),
            pltpu.VMEM((3, EDGE, chans), BF16),
            slabs,
            slabs,
            slabs,
            slabs,
            pieces,
            pieces,
            pltpu.VMEM((2, tiles, n_ctx, share, LANES), F32),
            pltpu.VMEM((3, tiles, n_ctx + GROUP - 1, share, LANES), F32),
            pltpu.VMEM((n_ctx * share, 2 * seg), BF16),
            pltpu.VMEM((seg, chans), F32),
            pltpu.VMEM((seg, chans), F32),
            pltpu.VMEM((n_ch, CHUNKS, step, chans), BF16),
            pltpu.VMEM((CHUNKS, step, cols), F32),
            pltpu.VMEM((seg, cols), BF16),
            dma((6,)),
            dma((2,)),
            dma((2,)),
            dma((2,)),
            dma((CHUNKS, 2)),
            dma((2,)),
            dma((2,)),
            dma((CHUNKS, 8)),
            dma((CHUNKS, 8)),
            dma((CHUNKS,)),
        ],
        compiler_params=pltpu.CompilerParams(
            collective_id=0, has_side_effects=True, vmem_limit_bytes=67043328
        ),
        name="hyena_operator",
    )(
        jnp.transpose(streams, (1, 0, 2)),
        short_taps,
        filters,
        skip_gain[None],
        table,
        out_weight,
    )


def solution(mesh):
    seg = 16384 // mesh.shape["ctx"]
    return jax.shard_map(
        functools.partial(local, table=half_table(2 * seg)),
        mesh=mesh,
        in_specs=(
            P("ctx", None, "ch"),
            P(None, None, "ch"),
            P("ctx", "ch"),
            P("ch"),
            P("ch", None),
        ),
        out_specs=P("ctx", "ch"),
        check_vma=False,
    )
```

```python
import functools

import jax
import jax.numpy as jnp
import ml_dtypes
import numpy as np
from jax import lax
from jax.experimental import pallas as pl
from jax.experimental.pallas import tpu as pltpu
from jax.sharding import PartitionSpec as P

LANES = 128
GROUP = 4
SPLITS = (1, 1, 1, 1)
HALVES = 2
LEAD = 2 * GROUP - 1
RING = 4
EDGE = 16
MESH = pl.DeviceIdType.MESH
F32 = jnp.float32
BF16 = jnp.bfloat16


def half_table(size):
    half = size // 2
    rows = np.arange(half, dtype=np.int64)[:, None]
    cols = np.arange(size, dtype=np.int64)[None, :]
    freq = np.where(cols < half, cols, cols - half)
    angle = (rows * freq % size).astype(np.float64) * (2.0 * np.pi / size)
    nyquist = np.where(rows % 2 == 0, 1.0, -1.0)
    table = np.where(cols < half, np.cos(angle), np.where(cols == half, nyquist, -np.sin(angle)))
    return table.astype(ml_dtypes.bfloat16)


def rows_of(ref):
    blocks, chans, width = ref.shape
    return ref[...].astype(F32).reshape(blocks * chans, width).astype(BF16)


def source_spectra(x_ref, table, xs):
    blocks, chans, half = x_ref.shape
    spec = jnp.dot(rows_of(x_ref), table[...], preferred_element_type=F32)
    lane = lax.broadcasted_iota(jnp.int32, (1, 1, LANES), 2)
    for q in range(half // LANES):
        real, imag = (
            spec[:, at : at + LANES].reshape(blocks, chans, LANES)
            for at in (q * LANES, half + q * LANES)
        )
        xs[0, q] = real + imag
        if q == 0:
            inside = jnp.broadcast_to(lane > 0, real.shape)
            real, imag = jnp.where(inside, real, imag), jnp.where(inside, imag, real)
        xs[1, q] = real
        xs[2, q] = imag


def filter_spectra(h_ref, table, hs):
    blocks, chans, half = h_ref.shape
    size = 2 * half
    filt = jnp.dot(rows_of(h_ref), table[...], preferred_element_type=F32)
    lane = lax.broadcasted_iota(jnp.int32, (1, 1, LANES), 2)
    for q in range(half // LANES):
        inside = (lane > 0) if q == 0 else (lane >= 0)
        weight = jnp.where(inside, 2.0 / size, 1.0 / size).astype(F32)
        signed = jnp.where(lane % 2 == 0, weight, -weight)
        parts = []
        for part in range(2):
            at = part * half + q * LANES
            block = filt[:, at : at + LANES].reshape(blocks, chans, LANES)
            before = jnp.concatenate(
                [jnp.zeros((1, chans, LANES), F32), block[: blocks - 1]], axis=0
            )
            parts.append(before * signed + block * weight)
        real, imag = parts
        terms = (real, imag - real, imag + real)
        if q == 0:
            keep = jnp.broadcast_to(inside, real.shape)
            lone = (0.0, imag, -real)
            terms = tuple(jnp.where(keep, t, e) for t, e in zip(terms, lone, strict=True))
        for kind in range(3):
            hs[kind, q, LEAD:] = terms[kind]
            hs[kind, q, :LEAD] = jnp.zeros((LEAD, chans, LANES), F32)


def block_products(parity, xs, hs, low):
    _, tiles, blocks, chans, _ = xs.shape
    half = tiles * LANES

    def one_tile(q, _):
        def one_group(big, _):
            def one_source(small, total):
                total = list(total)
                for b in range(2):
                    gap = 2 * GROUP * (big - small) + 1 + parity - b
                    for kind in range(3):
                        x = [xs[kind, q, 2 * (GROUP * small + j) + b] for j in range(GROUP)]
                        g = [hs[kind, q, gap + 2 * m] for m in range(2 * GROUP - 1)]
                        for i in range(GROUP):
                            for j in range(GROUP):
                                total[kind * GROUP + i] += x[j] * g[i - j + GROUP - 1]
                return tuple(total)

            zero = jnp.zeros((chans, LANES), F32)
            total = lax.fori_loop(0, big + 1, one_source, (zero,) * (3 * GROUP))
            rows = pl.ds(pl.multiple_of(big * GROUP * chans, GROUP * chans), GROUP * chans)
            both, second, third = (total[k * GROUP : (k + 1) * GROUP] for k in range(3))
            real = [p - r for p, r in zip(both, third, strict=True)]
            imag = [p + r for p, r in zip(both, second, strict=True)]
            for part, value in enumerate((real, imag)):
                cols = pl.ds(pl.multiple_of(part * half + q * LANES, LANES), LANES)
                low[parity, rows, cols] = jnp.concatenate(value, axis=0).astype(BF16)
            return 0

        return lax.fori_loop(0, blocks // (2 * GROUP), one_group, 0)

    lax.fori_loop(0, tiles, one_tile, 0)


def take(sem, ref):
    pltpu.make_async_copy(ref, ref, sem).wait()


def operator_kernel(
    n_ctx,
    n_ch,
    streams,
    taps_in,
    filters,
    skip_in,
    table_in,
    weight,
    out,
    strm,
    taps,
    filt,
    skip,
    table,
    wide,
    pad,
    halo,
    send_h,
    recv_h,
    send_x,
    recv_x,
    send_y,
    recv_y,
    xs,
    hs,
    low,
    outer,
    direct,
    gat,
    give,
    gain,
    acc,
    out_v,
    local_sem,
    halo_sem,
    h_sem,
    x_sem,
    y_sem,
    w_sem,
    f_sem,
    g_send,
    g_recv,
    p_sem,
    out_sem,
):
    me = lax.axis_index("ctx")
    col = lax.axis_index("ch")
    core = lax.rem(me, 2)
    partner = me + 1 - 2 * core
    _, seg, chans = streams.shape
    share = chans // n_ctx
    cols = weight.shape[1] // n_ch
    rows = chans // 2

    base = RING * lax.div(col, RING)
    place = lax.rem(col, RING)
    r_place, l_place, f_place = (lax.rem(place + d, RING) for d in (1, RING - 1, 2))
    right, left = base + r_place, base + l_place
    across = col + RING - 2 * base

    def columns(block):
        return pl.ds(pl.multiple_of(block * cols, cols), cols)

    loads = [
        pltpu.make_async_copy(filters, filt, local_sem.at[0]),
        pltpu.make_async_copy(streams, strm, local_sem.at[1]),
        pltpu.make_async_copy(taps_in, taps, local_sem.at[2]),
        pltpu.make_async_copy(skip_in, skip, local_sem.at[3]),
        pltpu.make_async_copy(table_in, table, local_sem.at[4]),
        pltpu.make_async_copy(weight.at[:, columns(col)], wide.at[place, 0], local_sem.at[5]),
        pltpu.make_async_copy(weight.at[:, columns(across)], wide.at[place, 1], local_sem.at[6]),
    ]
    for load in loads:
        load.start()

    barrier = pltpu.get_barrier_semaphore()

    def greet_ctx(k, _):
        pl.semaphore_signal(
            barrier, inc=1, device_id={"ctx": lax.rem(me + k, n_ctx)}, device_id_type=MESH
        )
        return 0

    def greet_ch(k, _):
        pl.semaphore_signal(
            barrier, inc=1, device_id={"ch": lax.rem(col + k, n_ch)}, device_id_type=MESH
        )
        return 0

    lax.fori_loop(1, n_ctx, greet_ctx, 0)
    lax.fori_loop(1, n_ch, greet_ch, 0)

    piece = min(LANES, seg)

    def mix(at):
        def mixed(q):
            total = taps[0, q : q + 1] * pad[q, 8 + at : 8 + at + piece]
            total = total + taps[1, q : q + 1] * pad[q, 7 + at : 7 + at + piece]
            return total + taps[2, q : q + 1] * pad[q, 6 + at : 6 + at + piece]

        inner = (mixed(0) * mixed(1)).astype(BF16).astype(F32)
        send_x[:, :, at : at + piece] = inner.T.reshape(n_ctx, share, piece).astype(BF16)
        direct[at : at + piece] = skip[...] * inner
        outer[at : at + piece] = mixed(2)

    loads[0].wait()
    send_h[...] = filt[...].astype(F32).T.reshape(n_ctx, share, seg).astype(BF16)
    recv_h[me] = send_h[me]
    for load in loads[1:4]:
        load.wait()
    for q in range(3):
        pad[q, 8:] = strm[q].astype(F32)
    for at in range(piece, seg, piece):
        mix(at)
    pl.semaphore_wait(barrier, n_ctx - 1 + n_ch - 1)

    edge = pltpu.make_async_remote_copy(
        src_ref=streams.at[:, pl.ds(seg - EDGE, EDGE), :],
        dst_ref=halo,
        send_sem=halo_sem.at[0],
        recv_sem=halo_sem.at[1],
        device_id={"ctx": lax.rem(me + 1, n_ctx)},
        device_id_type=MESH,
    )
    edge.start()

    def slab(source, target, sem, there):
        pltpu.make_async_remote_copy(
            src_ref=source,
            dst_ref=target.at[me],
            send_sem=sem.at[0],
            recv_sem=sem.at[1],
            device_id={"ctx": there},
            device_id_type=MESH,
        ).start()

    def exchange(source, target, sem):
        def one(k, _):
            reach = lax.div(k + 1, 2)
            there = lax.rem(me + jnp.where(lax.rem(k, 2) == 1, reach, n_ctx - reach), n_ctx)
            slab(source.at[there], target, sem, there)
            return 0

        lax.fori_loop(1, n_ctx, one, 0)

    exchange(send_h, recv_h, h_sem)
    edge.wait_recv()
    pad[:, :8] = jnp.where(me > 0, halo[...].astype(F32)[:, EDGE - 8 :], 0.0)
    mix(0)
    recv_x[me] = send_x[me]
    exchange(send_x, recv_x, x_sem)

    half_rows = pl.ds(pl.multiple_of(core * rows, rows), rows)

    def lend(k, _):
        there = lax.rem(place + k, RING)
        for side, block in enumerate((base + there, across - place + there)):
            pltpu.make_async_remote_copy(
                src_ref=weight.at[half_rows, columns(block)],
                dst_ref=wide.at[place, side, half_rows],
                send_sem=w_sem.at[0],
                recv_sem=w_sem.at[1],
                device_id={"ch": base + there},
                device_id_type=MESH,
            ).start()
        return 0

    lax.fori_loop(1, RING, lend, 0)

    loads[4].wait()
    others = pl.ds(0, n_ctx - 1)
    take(h_sem.at[1], recv_h.at[others])
    filter_spectra(recv_h, table, hs)
    take(x_sem.at[1], recv_x.at[others])
    source_spectra(recv_x, table, xs)
    pairs = n_ctx // 2
    mine = lax.div(me, 2)
    wing = seg // HALVES
    for parity in range(2):
        block_products(parity, xs, hs, low)
        for side in range(HALVES):
            part = lax.dot_general(
                low[parity],
                table[side * wing : (side + 1) * wing],
                (((1,), (1,)), ((), ())),
                preferred_element_type=F32,
            )
            send_y[side, parity] = part.reshape(pairs, share, wing).astype(BF16)

            def back(k, _, side=side, parity=parity):
                reach = lax.div(k + 1, 2)
                pair = lax.rem(mine + jnp.where(lax.rem(k, 2) == 1, reach, pairs - reach), pairs)
                there = 2 * pair + parity

                @pl.when(there != me)
                def _():
                    slab(
                        send_y.at[side, parity, pair], recv_y.at[side], y_sem.at[side], there
                    )

                return 0

            lax.fori_loop(0, pairs, back, 0)
    for side in range(HALVES):
        recv_y[side, me] = send_y[side, core, mine]

    lent = wide.at[pl.ds(0, RING - 1), :, pl.ds(0, rows)]
    take(w_sem.at[1], lent)

    def pass_on(k, _):
        there = lax.rem(place + k, RING)
        pltpu.make_async_remote_copy(
            src_ref=wide.at[there, :, half_rows],
            dst_ref=wide.at[there, :, half_rows],
            send_sem=f_sem.at[0],
            recv_sem=f_sem.at[1],
            device_id={"ctx": partner},
            device_id_type=MESH,
        ).start()
        return 0

    lax.fori_loop(1, RING, pass_on, 0)

    unit = seg // sum(SPLITS)
    starts = [unit * sum(SPLITS[:kk]) for kk in range(len(SPLITS))]
    sizes = [unit * split for split in SPLITS]
    last = len(SPLITS) - 1
    full = [pl.ds(at, size) for at, size in zip(starts, sizes, strict=True)]
    first = [pl.ds(at, size // 2) for at, size in zip(starts, sizes, strict=True)]
    second = [pl.ds(at + size // 2, size // 2) for at, size in zip(starts, sizes, strict=True)]

    def hop(kk, kind, block, spans, there):
        span = spans[kk]
        return pltpu.make_async_remote_copy(
            src_ref=gat.at[block, span],
            dst_ref=gat.at[block, span],
            send_sem=g_send.at[kk, kind],
            recv_sem=g_recv.at[kk, kind],
            device_id={"ch": there},
            device_id_type=MESH,
        )

    sent = []

    def push(copy):
        copy.start()
        sent.append(copy)

    def begin(kk):
        at, size = starts[kk], sizes[kk]
        side, inside = at // wing, at % wing
        if inside == 0:
            take(y_sem.at[side, 1], recv_y.at[side, others])
        conv = recv_y[side, :, :, inside : inside + size].astype(F32).reshape(chans, size).T
        gated = outer[full[kk]] * (conv + direct[full[kk]])
        gat[place, full[kk]] = gated.astype(BF16)
        push(hop(kk, 0, place, full, right))
        push(hop(kk, 1, place, full, left))
        push(hop(kk, 2, place, full, base + f_place))

    def relay(kk):
        hop(kk, 0, l_place, full, left).wait_recv()
        hop(kk, 1, r_place, full, right).wait_recv()

    def partial(kk, side):
        total = jnp.dot(gat[place, full[kk]], wide[place, side], preferred_element_type=F32)
        for block in (l_place, r_place, f_place):
            total += jnp.dot(gat[block, full[kk]], wide[block, side], preferred_element_type=F32)
        return total

    def share_out(kk):
        return pltpu.make_async_remote_copy(
            src_ref=give.at[full[kk]],
            dst_ref=gain.at[full[kk]],
            send_sem=p_sem.at[0, kk],
            recv_sem=p_sem.at[1, kk],
            device_id={"ch": across},
            device_id_type=MESH,
        )

    def combine(kk):
        hop(kk, 2, f_place, full, left).wait_recv()
        give[full[kk]] = partial(kk, 1).astype(BF16)
        push(share_out(kk))
        acc[full[kk]] = partial(kk, 0)

    for kk in range(last + 1):
        begin(kk)
    loads[5].wait()
    loads[6].wait()
    take(f_sem.at[1], lent)
    for kk in range(last + 1):
        relay(kk)
        combine(kk)
    stores = []
    for kk in range(last + 1):
        share_out(kk).wait_recv()
        span = full[kk]
        out_v[span] = (acc[span] + gain[span].astype(F32)).astype(BF16)
        stores.append(pltpu.make_async_copy(out_v.at[span], out.at[span], out_sem.at[kk]))
        stores[-1].start()

    edge.wait_send()
    take(h_sem.at[0], send_h.at[others])
    take(x_sem.at[0], send_x.at[others])
    for side in range(HALVES):
        take(y_sem.at[side, 0], recv_y.at[side, others])
    take(w_sem.at[0], lent)
    take(f_sem.at[0], lent)
    for copy in sent:
        copy.wait_send()
    for store in stores:
        store.wait()


def local(streams, short_taps, filters, skip_gain, out_weight, *, table):
    n_ctx, n_ch = lax.axis_size("ctx"), lax.axis_size("ch")
    seg, _, chans = streams.shape
    share = chans // n_ctx
    cols = out_weight.shape[1] // n_ch
    tiles = seg // LANES
    slabs = pltpu.VMEM((n_ctx, share, seg), BF16)
    wing = seg // HALVES
    parts = pltpu.VMEM((seg, cols), BF16)
    chunks = len(SPLITS)
    dma = pltpu.SemaphoreType.DMA
    return pl.pallas_call(
        functools.partial(operator_kernel, n_ctx, n_ch),
        out_shape=jax.ShapeDtypeStruct((seg, cols), BF16),
        in_specs=[pl.BlockSpec(memory_space=pl.ANY)] * 6,
        out_specs=pl.BlockSpec(memory_space=pl.ANY),
        scratch_shapes=[
            pltpu.VMEM((3, seg, chans), BF16),
            pltpu.VMEM(short_taps.shape, F32),
            pltpu.VMEM((seg, chans), BF16),
            pltpu.VMEM((1, chans), F32),
            pltpu.VMEM((seg, 2 * seg), BF16),
            pltpu.VMEM((RING, 2, chans, cols), BF16),
            pltpu.VMEM((3, seg + 8, chans), F32),
            pltpu.VMEM((3, EDGE, chans), BF16),
            slabs,
            slabs,
            slabs,
            slabs,
            pltpu.VMEM((HALVES, 2, n_ctx // 2, share, wing), BF16),
            pltpu.VMEM((HALVES, n_ctx, share, wing), BF16),
            pltpu.VMEM((3, tiles, n_ctx, share, LANES), F32),
            pltpu.VMEM((3, tiles, n_ctx + LEAD, share, LANES), F32),
            pltpu.VMEM((2, n_ctx // 2 * share, 2 * seg), BF16),
            pltpu.VMEM((seg, chans), F32),
            pltpu.VMEM((seg, chans), F32),
            pltpu.VMEM((RING, seg, chans), BF16),
            parts,
            parts,
            pltpu.VMEM((seg, cols), F32),
            pltpu.VMEM((seg, cols), BF16),
            dma((7,)),
            dma((2,)),
            dma((2,)),
            dma((2,)),
            dma((HALVES, 2)),
            dma((2,)),
            dma((2,)),
            dma((chunks, 4)),
            dma((chunks, 4)),
            dma((2, chunks)),
            dma((chunks,)),
        ],
        compiler_params=pltpu.CompilerParams(
            collective_id=0, has_side_effects=True, vmem_limit_bytes=67043328
        ),
        name="hyena_operator",
    )(
        jnp.transpose(streams, (1, 0, 2)),
        short_taps,
        filters,
        skip_gain[None],
        table,
        out_weight,
    )


def solution(mesh):
    seg = 16384 // mesh.shape["ctx"]
    return jax.shard_map(
        functools.partial(local, table=half_table(2 * seg)),
        mesh=mesh,
        in_specs=(
            P("ctx", None, "ch"),
            P(None, None, "ch"),
            P("ctx", "ch"),
            P("ch"),
            P("ch", None),
        ),
        out_specs=P("ctx", "ch"),
        check_vma=False,
    )
```

```python
import functools

import jax
import jax.numpy as jnp
import ml_dtypes
import numpy as np
from jax import lax
from jax.experimental import pallas as pl
from jax.experimental.pallas import tpu as pltpu
from jax.sharding import PartitionSpec as P

LANES = 128
GROUP = 4
SPLITS = (1, 1, 1, 1)
HALVES = 2
LEAD = 2 * GROUP - 1
RING = 4
EDGE = 16
MESH = pl.DeviceIdType.MESH
F32 = jnp.float32
BF16 = jnp.bfloat16


def half_table(size):
    half = size // 2
    rows = np.arange(half, dtype=np.int64)[:, None]
    cols = np.arange(size, dtype=np.int64)[None, :]
    freq = np.where(cols < half, cols, cols - half)
    angle = (rows * freq % size).astype(np.float64) * (2.0 * np.pi / size)
    nyquist = np.where(rows % 2 == 0, 1.0, -1.0)
    table = np.where(cols < half, np.cos(angle), np.where(cols == half, nyquist, -np.sin(angle)))
    return table.astype(ml_dtypes.bfloat16)


def rows_of(ref):
    blocks, chans, width = ref.shape
    return ref[...].astype(F32).reshape(blocks * chans, width).astype(BF16)


def source_spectra(x_ref, table, xs):
    blocks, chans, half = x_ref.shape
    spec = jnp.dot(rows_of(x_ref), table[...], preferred_element_type=F32)
    lane = lax.broadcasted_iota(jnp.int32, (1, 1, LANES), 2)
    for q in range(half // LANES):
        real, imag = (
            spec[:, at : at + LANES].reshape(blocks, chans, LANES)
            for at in (q * LANES, half + q * LANES)
        )
        xs[0, q] = real + imag
        if q == 0:
            inside = jnp.broadcast_to(lane > 0, real.shape)
            real, imag = jnp.where(inside, real, imag), jnp.where(inside, imag, real)
        xs[1, q] = real
        xs[2, q] = imag


def filter_spectra(h_ref, table, hs):
    blocks, chans, half = h_ref.shape
    size = 2 * half
    filt = jnp.dot(rows_of(h_ref), table[...], preferred_element_type=F32)
    lane = lax.broadcasted_iota(jnp.int32, (1, 1, LANES), 2)
    for q in range(half // LANES):
        inside = (lane > 0) if q == 0 else (lane >= 0)
        weight = jnp.where(inside, 2.0 / size, 1.0 / size).astype(F32)
        signed = jnp.where(lane % 2 == 0, weight, -weight)
        parts = []
        for part in range(2):
            at = part * half + q * LANES
            block = filt[:, at : at + LANES].reshape(blocks, chans, LANES)
            before = jnp.concatenate(
                [jnp.zeros((1, chans, LANES), F32), block[: blocks - 1]], axis=0
            )
            parts.append(before * signed + block * weight)
        real, imag = parts
        terms = (real, imag - real, imag + real)
        if q == 0:
            keep = jnp.broadcast_to(inside, real.shape)
            lone = (0.0, imag, -real)
            terms = tuple(jnp.where(keep, t, e) for t, e in zip(terms, lone, strict=True))
        for kind in range(3):
            hs[kind, q, LEAD:] = terms[kind]
            hs[kind, q, :LEAD] = jnp.zeros((LEAD, chans, LANES), F32)


def block_products(parity, xs, hs, low):
    _, tiles, blocks, chans, _ = xs.shape
    half = tiles * LANES

    def one_tile(q, _):
        def one_group(big, _):
            def one_source(small, total):
                total = list(total)
                for b in range(2):
                    gap = 2 * GROUP * (big - small) + 1 + parity - b
                    for kind in range(3):
                        x = [xs[kind, q, 2 * (GROUP * small + j) + b] for j in range(GROUP)]
                        g = [hs[kind, q, gap + 2 * m] for m in range(2 * GROUP - 1)]
                        for i in range(GROUP):
                            for j in range(GROUP):
                                total[kind * GROUP + i] += x[j] * g[i - j + GROUP - 1]
                return tuple(total)

            zero = jnp.zeros((chans, LANES), F32)
            total = lax.fori_loop(0, big + 1, one_source, (zero,) * (3 * GROUP))
            rows = pl.ds(pl.multiple_of(big * GROUP * chans, GROUP * chans), GROUP * chans)
            both, second, third = (total[k * GROUP : (k + 1) * GROUP] for k in range(3))
            real = [p - r for p, r in zip(both, third, strict=True)]
            imag = [p + r for p, r in zip(both, second, strict=True)]
            for part, value in enumerate((real, imag)):
                cols = pl.ds(pl.multiple_of(part * half + q * LANES, LANES), LANES)
                low[parity, rows, cols] = jnp.concatenate(value, axis=0).astype(BF16)
            return 0

        return lax.fori_loop(0, blocks // (2 * GROUP), one_group, 0)

    lax.fori_loop(0, tiles, one_tile, 0)


def take(sem, ref):
    pltpu.make_async_copy(ref, ref, sem).wait()


def operator_kernel(
    n_ctx,
    n_ch,
    streams,
    taps_in,
    filters,
    skip_in,
    table_in,
    weight,
    out,
    strm,
    taps,
    filt,
    skip,
    table,
    wide,
    pad,
    halo,
    send_h,
    recv_h,
    send_x,
    recv_x,
    send_y,
    recv_y,
    xs,
    hs,
    low,
    outer,
    direct,
    gat,
    give,
    gain,
    acc,
    out_v,
    local_sem,
    halo_sem,
    h_sem,
    x_sem,
    y_sem,
    w_sem,
    f_sem,
    g_send,
    g_recv,
    p_sem,
    out_sem,
):
    me = lax.axis_index("ctx")
    col = lax.axis_index("ch")
    core = lax.rem(me, 2)
    partner = me + 1 - 2 * core
    _, seg, chans = streams.shape
    share = chans // n_ctx
    cols = weight.shape[1] // n_ch
    rows = chans // 2

    base = RING * lax.div(col, RING)
    place = lax.rem(col, RING)
    r_place, l_place, f_place = (lax.rem(place + d, RING) for d in (1, RING - 1, 2))
    right, left = base + r_place, base + l_place
    across = col + RING - 2 * base

    def columns(block):
        return pl.ds(pl.multiple_of(block * cols, cols), cols)

    loads = [
        pltpu.make_async_copy(filters, filt, local_sem.at[0]),
        pltpu.make_async_copy(streams, strm, local_sem.at[1]),
        pltpu.make_async_copy(taps_in, taps, local_sem.at[2]),
        pltpu.make_async_copy(skip_in, skip, local_sem.at[3]),
        pltpu.make_async_copy(table_in, table, local_sem.at[4]),
        pltpu.make_async_copy(weight.at[:, columns(col)], wide.at[place, 0], local_sem.at[5]),
        pltpu.make_async_copy(weight.at[:, columns(across)], wide.at[place, 1], local_sem.at[6]),
    ]
    for load in loads:
        load.start()

    barrier = pltpu.get_barrier_semaphore()

    def greet_ctx(k, _):
        pl.semaphore_signal(
            barrier, inc=1, device_id={"ctx": lax.rem(me + k, n_ctx)}, device_id_type=MESH
        )
        return 0

    def greet_ch(k, _):
        pl.semaphore_signal(
            barrier, inc=1, device_id={"ch": lax.rem(col + k, n_ch)}, device_id_type=MESH
        )
        return 0

    lax.fori_loop(1, n_ctx, greet_ctx, 0)
    lax.fori_loop(1, n_ch, greet_ch, 0)

    piece = min(LANES, seg)

    def mix(at):
        def mixed(q):
            total = taps[0, q : q + 1] * pad[q, 8 + at : 8 + at + piece]
            total = total + taps[1, q : q + 1] * pad[q, 7 + at : 7 + at + piece]
            return total + taps[2, q : q + 1] * pad[q, 6 + at : 6 + at + piece]

        inner = (mixed(0) * mixed(1)).astype(BF16).astype(F32)
        send_x[:, :, at : at + piece] = inner.T.reshape(n_ctx, share, piece).astype(BF16)
        direct[at : at + piece] = skip[...] * inner
        outer[at : at + piece] = mixed(2)

    loads[0].wait()
    send_h[...] = filt[...].astype(F32).T.reshape(n_ctx, share, seg).astype(BF16)
    recv_h[me] = send_h[me]
    for load in loads[1:4]:
        load.wait()
    for q in range(3):
        pad[q, 8:] = strm[q].astype(F32)
    for at in range(piece, seg, piece):
        mix(at)
    pl.semaphore_wait(barrier, n_ctx - 1 + n_ch - 1)

    edge = pltpu.make_async_remote_copy(
        src_ref=streams.at[:, pl.ds(seg - EDGE, EDGE), :],
        dst_ref=halo,
        send_sem=halo_sem.at[0],
        recv_sem=halo_sem.at[1],
        device_id={"ctx": lax.rem(me + 1, n_ctx)},
        device_id_type=MESH,
    )
    edge.start()

    def slab(source, target, sem, there):
        pltpu.make_async_remote_copy(
            src_ref=source,
            dst_ref=target.at[me],
            send_sem=sem.at[0],
            recv_sem=sem.at[1],
            device_id={"ctx": there},
            device_id_type=MESH,
        ).start()

    def reach(k, count):
        turn, spot = lax.div(k + 1, 4), lax.rem(k + 1, 4)
        ahead = count // 4 + jnp.where(spot < 2, turn, -turn)
        return jnp.where(lax.rem(spot, 2) == 0, ahead, count - ahead)

    def exchange(source, target, sem):
        def one(k, _):
            there = lax.rem(me + reach(k, n_ctx), n_ctx)
            slab(source.at[there], target, sem, there)
            return 0

        lax.fori_loop(1, n_ctx, one, 0)

    exchange(send_h, recv_h, h_sem)
    edge.wait_recv()
    pad[:, :8] = jnp.where(me > 0, halo[...].astype(F32)[:, EDGE - 8 :], 0.0)
    mix(0)
    recv_x[me] = send_x[me]
    exchange(send_x, recv_x, x_sem)

    half_rows = pl.ds(pl.multiple_of(core * rows, rows), rows)

    def lend(k, _):
        there = lax.rem(place + k, RING)
        for side, block in enumerate((base + there, across - place + there)):
            pltpu.make_async_remote_copy(
                src_ref=weight.at[half_rows, columns(block)],
                dst_ref=wide.at[place, side, half_rows],
                send_sem=w_sem.at[0],
                recv_sem=w_sem.at[1],
                device_id={"ch": base + there},
                device_id_type=MESH,
            ).start()
        return 0

    lax.fori_loop(1, RING, lend, 0)

    loads[4].wait()
    others = pl.ds(0, n_ctx - 1)
    take(h_sem.at[1], recv_h.at[others])
    filter_spectra(recv_h, table, hs)
    take(x_sem.at[1], recv_x.at[others])
    source_spectra(recv_x, table, xs)
    pairs = n_ctx // 2
    mine = lax.div(me, 2)
    wing = seg // HALVES
    for parity in range(2):
        block_products(parity, xs, hs, low)
        for side in range(HALVES):
            part = lax.dot_general(
                low[parity],
                table[side * wing : (side + 1) * wing],
                (((1,), (1,)), ((), ())),
                preferred_element_type=F32,
            )
            send_y[side, parity] = part.reshape(pairs, share, wing).astype(BF16)

            def back(k, _, side=side, parity=parity):
                pair = lax.rem(mine + jnp.where(k < pairs, reach(k, pairs), 0), pairs)
                there = 2 * pair + parity

                @pl.when(there != me)
                def _():
                    slab(
                        send_y.at[side, parity, pair], recv_y.at[side], y_sem.at[side], there
                    )

                return 0

            lax.fori_loop(1, pairs + 1, back, 0)
    for side in range(HALVES):
        recv_y[side, me] = send_y[side, core, mine]

    lent = wide.at[pl.ds(0, RING - 1), :, pl.ds(0, rows)]
    take(w_sem.at[1], lent)

    def pass_on(k, _):
        there = lax.rem(place + k, RING)
        pltpu.make_async_remote_copy(
            src_ref=wide.at[there, :, half_rows],
            dst_ref=wide.at[there, :, half_rows],
            send_sem=f_sem.at[0],
            recv_sem=f_sem.at[1],
            device_id={"ctx": partner},
            device_id_type=MESH,
        ).start()
        return 0

    lax.fori_loop(1, RING, pass_on, 0)

    unit = seg // sum(SPLITS)
    starts = [unit * sum(SPLITS[:kk]) for kk in range(len(SPLITS))]
    sizes = [unit * split for split in SPLITS]
    last = len(SPLITS) - 1
    full = [pl.ds(at, size) for at, size in zip(starts, sizes, strict=True)]
    first = [pl.ds(at, size // 2) for at, size in zip(starts, sizes, strict=True)]
    second = [pl.ds(at + size // 2, size // 2) for at, size in zip(starts, sizes, strict=True)]

    def hop(kk, kind, block, spans, there):
        span = spans[kk]
        return pltpu.make_async_remote_copy(
            src_ref=gat.at[block, span],
            dst_ref=gat.at[block, span],
            send_sem=g_send.at[kk, kind],
            recv_sem=g_recv.at[kk, kind],
            device_id={"ch": there},
            device_id_type=MESH,
        )

    sent = []

    def push(copy):
        copy.start()
        sent.append(copy)

    def begin(kk):
        at, size = starts[kk], sizes[kk]
        side, inside = at // wing, at % wing
        if inside == 0:
            take(y_sem.at[side, 1], recv_y.at[side, others])
        conv = recv_y[side, :, :, inside : inside + size].astype(F32).reshape(chans, size).T
        gated = outer[full[kk]] * (conv + direct[full[kk]])
        gat[place, full[kk]] = gated.astype(BF16)
        push(hop(kk, 0, place, full, right))
        push(hop(kk, 1, place, full, left))
        push(hop(kk, 2, place, full, base + f_place))

    def relay(kk):
        hop(kk, 0, l_place, full, left).wait_recv()
        hop(kk, 1, r_place, full, right).wait_recv()

    def partial(kk, side):
        total = jnp.dot(gat[place, full[kk]], wide[place, side], preferred_element_type=F32)
        for block in (l_place, r_place, f_place):
            total += jnp.dot(gat[block, full[kk]], wide[block, side], preferred_element_type=F32)
        return total

    def share_out(kk):
        return pltpu.make_async_remote_copy(
            src_ref=give.at[full[kk]],
            dst_ref=gain.at[full[kk]],
            send_sem=p_sem.at[0, kk],
            recv_sem=p_sem.at[1, kk],
            device_id={"ch": across},
            device_id_type=MESH,
        )

    def combine(kk):
        hop(kk, 2, f_place, full, left).wait_recv()
        give[full[kk]] = partial(kk, 1).astype(BF16)
        push(share_out(kk))
        acc[full[kk]] = partial(kk, 0)

    for kk in range(last + 1):
        begin(kk)
    loads[5].wait()
    loads[6].wait()
    take(f_sem.at[1], lent)
    for kk in range(last + 1):
        relay(kk)
        combine(kk)
    stores = []
    for kk in range(last + 1):
        share_out(kk).wait_recv()
        span = full[kk]
        out_v[span] = (acc[span] + gain[span].astype(F32)).astype(BF16)
        stores.append(pltpu.make_async_copy(out_v.at[span], out.at[span], out_sem.at[kk]))
        stores[-1].start()

    edge.wait_send()
    take(h_sem.at[0], send_h.at[others])
    take(x_sem.at[0], send_x.at[others])
    for side in range(HALVES):
        take(y_sem.at[side, 0], recv_y.at[side, others])
    take(w_sem.at[0], lent)
    take(f_sem.at[0], lent)
    for copy in sent:
        copy.wait_send()
    for store in stores:
        store.wait()


def local(streams, short_taps, filters, skip_gain, out_weight, *, table):
    n_ctx, n_ch = lax.axis_size("ctx"), lax.axis_size("ch")
    seg, _, chans = streams.shape
    share = chans // n_ctx
    cols = out_weight.shape[1] // n_ch
    tiles = seg // LANES
    slabs = pltpu.VMEM((n_ctx, share, seg), BF16)
    wing = seg // HALVES
    parts = pltpu.VMEM((seg, cols), BF16)
    chunks = len(SPLITS)
    dma = pltpu.SemaphoreType.DMA
    return pl.pallas_call(
        functools.partial(operator_kernel, n_ctx, n_ch),
        out_shape=jax.ShapeDtypeStruct((seg, cols), BF16),
        in_specs=[pl.BlockSpec(memory_space=pl.ANY)] * 6,
        out_specs=pl.BlockSpec(memory_space=pl.ANY),
        scratch_shapes=[
            pltpu.VMEM((3, seg, chans), BF16),
            pltpu.VMEM(short_taps.shape, F32),
            pltpu.VMEM((seg, chans), BF16),
            pltpu.VMEM((1, chans), F32),
            pltpu.VMEM((seg, 2 * seg), BF16),
            pltpu.VMEM((RING, 2, chans, cols), BF16),
            pltpu.VMEM((3, seg + 8, chans), F32),
            pltpu.VMEM((3, EDGE, chans), BF16),
            slabs,
            slabs,
            slabs,
            slabs,
            pltpu.VMEM((HALVES, 2, n_ctx // 2, share, wing), BF16),
            pltpu.VMEM((HALVES, n_ctx, share, wing), BF16),
            pltpu.VMEM((3, tiles, n_ctx, share, LANES), F32),
            pltpu.VMEM((3, tiles, n_ctx + LEAD, share, LANES), F32),
            pltpu.VMEM((2, n_ctx // 2 * share, 2 * seg), BF16),
            pltpu.VMEM((seg, chans), F32),
            pltpu.VMEM((seg, chans), F32),
            pltpu.VMEM((RING, seg, chans), BF16),
            parts,
            parts,
            pltpu.VMEM((seg, cols), F32),
            pltpu.VMEM((seg, cols), BF16),
            dma((7,)),
            dma((2,)),
            dma((2,)),
            dma((2,)),
            dma((HALVES, 2)),
            dma((2,)),
            dma((2,)),
            dma((chunks, 4)),
            dma((chunks, 4)),
            dma((2, chunks)),
            dma((chunks,)),
        ],
        compiler_params=pltpu.CompilerParams(
            collective_id=0, has_side_effects=True, vmem_limit_bytes=67043328
        ),
        name="hyena_operator",
    )(
        jnp.transpose(streams, (1, 0, 2)),
        short_taps,
        filters,
        skip_gain[None],
        table,
        out_weight,
    )


def solution(mesh):
    seg = 16384 // mesh.shape["ctx"]
    return jax.shard_map(
        functools.partial(local, table=half_table(2 * seg)),
        mesh=mesh,
        in_specs=(
            P("ctx", None, "ch"),
            P(None, None, "ch"),
            P("ctx", "ch"),
            P("ch"),
            P("ch", None),
        ),
        out_specs=P("ctx", "ch"),
        check_vma=False,
    )
```

```python
import functools

import jax
import jax.numpy as jnp
import ml_dtypes
import numpy as np
from jax import lax
from jax.experimental import pallas as pl
from jax.experimental.pallas import tpu as pltpu
from jax.sharding import PartitionSpec as P

LANES = 128
GROUP = 4
SPLITS = (1, 1, 1, 1)
HALVES = 2
LEAD = 2 * GROUP - 1
RING = 4
EDGE = 16
MESH = pl.DeviceIdType.MESH
F32 = jnp.float32
BF16 = jnp.bfloat16


def half_table(size):
    half = size // 2
    rows = np.arange(half, dtype=np.int64)[:, None]
    cols = np.arange(size, dtype=np.int64)[None, :]
    freq = np.where(cols < half, cols, cols - half)
    angle = (rows * freq % size).astype(np.float64) * (2.0 * np.pi / size)
    nyquist = np.where(rows % 2 == 0, 1.0, -1.0)
    table = np.where(cols < half, np.cos(angle), np.where(cols == half, nyquist, -np.sin(angle)))
    return table.astype(ml_dtypes.bfloat16)


def rows_of(ref):
    blocks, chans, width = ref.shape
    return ref[...].astype(F32).reshape(blocks * chans, width).astype(BF16)


def source_spectra(x_ref, table, xs):
    blocks, chans, half = x_ref.shape
    spec = jnp.dot(rows_of(x_ref), table[...], preferred_element_type=F32)
    lane = lax.broadcasted_iota(jnp.int32, (1, 1, LANES), 2)
    for q in range(half // LANES):
        real, imag = (
            spec[:, at : at + LANES].reshape(blocks, chans, LANES)
            for at in (q * LANES, half + q * LANES)
        )
        xs[0, q] = real + imag
        if q == 0:
            inside = jnp.broadcast_to(lane > 0, real.shape)
            real, imag = jnp.where(inside, real, imag), jnp.where(inside, imag, real)
        xs[1, q] = real
        xs[2, q] = imag


def filter_spectra(h_ref, table, hs):
    blocks, chans, half = h_ref.shape
    size = 2 * half
    filt = jnp.dot(rows_of(h_ref), table[...], preferred_element_type=F32)
    lane = lax.broadcasted_iota(jnp.int32, (1, 1, LANES), 2)
    for q in range(half // LANES):
        inside = (lane > 0) if q == 0 else (lane >= 0)
        weight = jnp.where(inside, 2.0 / size, 1.0 / size).astype(F32)
        signed = jnp.where(lane % 2 == 0, weight, -weight)
        parts = []
        for part in range(2):
            at = part * half + q * LANES
            block = filt[:, at : at + LANES].reshape(blocks, chans, LANES)
            before = jnp.concatenate(
                [jnp.zeros((1, chans, LANES), F32), block[: blocks - 1]], axis=0
            )
            parts.append(before * signed + block * weight)
        real, imag = parts
        terms = (real, imag - real, imag + real)
        if q == 0:
            keep = jnp.broadcast_to(inside, real.shape)
            lone = (0.0, imag, -real)
            terms = tuple(jnp.where(keep, t, e) for t, e in zip(terms, lone, strict=True))
        for kind in range(3):
            hs[kind, q, LEAD:] = terms[kind]
            hs[kind, q, :LEAD] = jnp.zeros((LEAD, chans, LANES), F32)


def block_products(parity, xs, hs, low):
    _, tiles, blocks, chans, _ = xs.shape
    half = tiles * LANES

    def one_tile(q, _):
        def one_group(big, _):
            def one_source(small, total):
                total = list(total)
                for b in range(2):
                    gap = 2 * GROUP * (big - small) + 1 + parity - b
                    for kind in range(3):
                        x = [xs[kind, q, 2 * (GROUP * small + j) + b] for j in range(GROUP)]
                        g = [hs[kind, q, gap + 2 * m] for m in range(2 * GROUP - 1)]
                        for i in range(GROUP):
                            for j in range(GROUP):
                                total[kind * GROUP + i] += x[j] * g[i - j + GROUP - 1]
                return tuple(total)

            zero = jnp.zeros((chans, LANES), F32)
            total = lax.fori_loop(0, big + 1, one_source, (zero,) * (3 * GROUP))
            rows = pl.ds(pl.multiple_of(big * GROUP * chans, GROUP * chans), GROUP * chans)
            both, second, third = (total[k * GROUP : (k + 1) * GROUP] for k in range(3))
            real = [p - r for p, r in zip(both, third, strict=True)]
            imag = [p + r for p, r in zip(both, second, strict=True)]
            for part, value in enumerate((real, imag)):
                cols = pl.ds(pl.multiple_of(part * half + q * LANES, LANES), LANES)
                low[parity, rows, cols] = jnp.concatenate(value, axis=0).astype(BF16)
            return 0

        return lax.fori_loop(0, blocks // (2 * GROUP), one_group, 0)

    lax.fori_loop(0, tiles, one_tile, 0)


def take(sem, ref):
    pltpu.make_async_copy(ref, ref, sem).wait()


def operator_kernel(
    n_ctx,
    n_ch,
    streams,
    taps_in,
    filters,
    skip_in,
    table_in,
    weight,
    own_out,
    gain,
    strm,
    taps,
    filt,
    skip,
    table,
    wide,
    pad,
    halo,
    send_h,
    recv_h,
    send_x,
    recv_x,
    send_y,
    recv_y,
    xs,
    hs,
    low,
    outer,
    direct,
    gat,
    give,
    acc,
    local_sem,
    halo_sem,
    h_sem,
    x_sem,
    y_sem,
    w_sem,
    f_sem,
    g_send,
    g_recv,
    p_sem,
    out_sem,
):
    me = lax.axis_index("ctx")
    col = lax.axis_index("ch")
    core = lax.rem(me, 2)
    partner = me + 1 - 2 * core
    _, seg, chans = streams.shape
    share = chans // n_ctx
    cols = weight.shape[1] // n_ch
    rows = chans // 2

    base = RING * lax.div(col, RING)
    place = lax.rem(col, RING)
    r_place, l_place, f_place = (lax.rem(place + d, RING) for d in (1, RING - 1, 2))
    right, left = base + r_place, base + l_place
    across = col + RING - 2 * base

    def columns(block):
        return pl.ds(pl.multiple_of(block * cols, cols), cols)

    loads = [
        pltpu.make_async_copy(filters, filt, local_sem.at[0]),
        pltpu.make_async_copy(streams, strm, local_sem.at[1]),
        pltpu.make_async_copy(taps_in, taps, local_sem.at[2]),
        pltpu.make_async_copy(skip_in, skip, local_sem.at[3]),
        pltpu.make_async_copy(table_in, table, local_sem.at[4]),
        pltpu.make_async_copy(weight.at[:, columns(col)], wide.at[place, 0], local_sem.at[5]),
        pltpu.make_async_copy(weight.at[:, columns(across)], wide.at[place, 1], local_sem.at[6]),
    ]
    for load in loads:
        load.start()

    barrier = pltpu.get_barrier_semaphore()

    def reach(k, count):
        turn, spot = lax.div(k + 1, 4), lax.rem(k + 1, 4)
        ahead = count // 4 + jnp.where(spot < 2, turn, -turn)
        return jnp.where(lax.rem(spot, 2) == 0, ahead, count - ahead)

    def greet_ctx(k, _):
        there = lax.rem(me + reach(k, n_ctx), n_ctx)
        pl.semaphore_signal(barrier, inc=1, device_id={"ctx": there}, device_id_type=MESH)
        return 0

    def greet_ch(k, _):
        pl.semaphore_signal(
            barrier, inc=1, device_id={"ch": lax.rem(col + k, n_ch)}, device_id_type=MESH
        )
        return 0

    lax.fori_loop(1, n_ctx, greet_ctx, 0)
    lax.fori_loop(1, n_ch, greet_ch, 0)

    piece = min(LANES, seg)

    def mix(at):
        def mixed(q):
            total = taps[0, q : q + 1] * pad[q, 8 + at : 8 + at + piece]
            total = total + taps[1, q : q + 1] * pad[q, 7 + at : 7 + at + piece]
            return total + taps[2, q : q + 1] * pad[q, 6 + at : 6 + at + piece]

        inner = (mixed(0) * mixed(1)).astype(BF16).astype(F32)
        send_x[:, :, at : at + piece] = inner.T.reshape(n_ctx, share, piece).astype(BF16)
        direct[at : at + piece] = skip[...] * inner
        outer[at : at + piece] = mixed(2)

    loads[0].wait()
    send_h[...] = filt[...].astype(F32).T.reshape(n_ctx, share, seg).astype(BF16)
    recv_h[me] = send_h[me]
    for load in loads[1:4]:
        load.wait()
    for q in range(3):
        pad[q, 8:] = strm[q].astype(F32)
    for at in range(piece, seg, piece):
        mix(at)
    pl.semaphore_wait(barrier, n_ctx - 1 + n_ch - 1)

    edge = pltpu.make_async_remote_copy(
        src_ref=streams.at[:, pl.ds(seg - EDGE, EDGE), :],
        dst_ref=halo,
        send_sem=halo_sem.at[0],
        recv_sem=halo_sem.at[1],
        device_id={"ctx": lax.rem(me + 1, n_ctx)},
        device_id_type=MESH,
    )
    edge.start()

    def slab(source, target, sem, there):
        pltpu.make_async_remote_copy(
            src_ref=source,
            dst_ref=target.at[me],
            send_sem=sem.at[0],
            recv_sem=sem.at[1],
            device_id={"ctx": there},
            device_id_type=MESH,
        ).start()

    def exchange(source, target, sem):
        def one(k, _):
            there = lax.rem(me + reach(k, n_ctx), n_ctx)
            slab(source.at[there], target, sem, there)
            return 0

        lax.fori_loop(1, n_ctx, one, 0)

    exchange(send_h, recv_h, h_sem)
    edge.wait_recv()
    pad[:, :8] = jnp.where(me > 0, halo[...].astype(F32)[:, EDGE - 8 :], 0.0)
    mix(0)
    recv_x[me] = send_x[me]
    exchange(send_x, recv_x, x_sem)

    half_rows = pl.ds(pl.multiple_of(core * rows, rows), rows)

    def lend(k, _):
        there = lax.rem(place + k, RING)
        for side, block in enumerate((base + there, across - place + there)):
            pltpu.make_async_remote_copy(
                src_ref=weight.at[half_rows, columns(block)],
                dst_ref=wide.at[place, side, half_rows],
                send_sem=w_sem.at[0],
                recv_sem=w_sem.at[1],
                device_id={"ch": base + there},
                device_id_type=MESH,
            ).start()
        return 0

    lax.fori_loop(1, RING, lend, 0)

    loads[4].wait()
    others = pl.ds(0, n_ctx - 1)
    take(h_sem.at[1], recv_h.at[others])
    filter_spectra(recv_h, table, hs)
    take(x_sem.at[1], recv_x.at[others])
    source_spectra(recv_x, table, xs)
    pairs = n_ctx // 2
    mine = lax.div(me, 2)
    wing = seg // HALVES
    for parity in range(2):
        block_products(parity, xs, hs, low)
        for side in range(HALVES):
            part = lax.dot_general(
                low[parity],
                table[side * wing : (side + 1) * wing],
                (((1,), (1,)), ((), ())),
                preferred_element_type=F32,
            )
            send_y[side, parity] = part.reshape(pairs, share, wing).astype(BF16)

            def back(k, _, side=side, parity=parity):
                pair = lax.rem(mine + jnp.where(k < pairs, reach(k, pairs), 0), pairs)
                there = 2 * pair + parity

                @pl.when(there != me)
                def _():
                    slab(
                        send_y.at[side, parity, pair], recv_y.at[side], y_sem.at[side], there
                    )

                return 0

            lax.fori_loop(1, pairs + 1, back, 0)
    for side in range(HALVES):
        recv_y[side, me] = send_y[side, core, mine]

    lent = wide.at[pl.ds(0, RING - 1), :, pl.ds(0, rows)]
    take(w_sem.at[1], lent)

    def pass_on(k, _):
        there = lax.rem(place + k, RING)
        pltpu.make_async_remote_copy(
            src_ref=wide.at[there, :, half_rows],
            dst_ref=wide.at[there, :, half_rows],
            send_sem=f_sem.at[0],
            recv_sem=f_sem.at[1],
            device_id={"ctx": partner},
            device_id_type=MESH,
        ).start()
        return 0

    lax.fori_loop(1, RING, pass_on, 0)

    unit = seg // sum(SPLITS)
    starts = [unit * sum(SPLITS[:kk]) for kk in range(len(SPLITS))]
    sizes = [unit * split for split in SPLITS]
    last = len(SPLITS) - 1
    full = [pl.ds(at, size) for at, size in zip(starts, sizes, strict=True)]
    first = [pl.ds(at, size // 2) for at, size in zip(starts, sizes, strict=True)]
    second = [pl.ds(at + size // 2, size // 2) for at, size in zip(starts, sizes, strict=True)]

    def hop(kk, kind, block, spans, there):
        span = spans[kk]
        return pltpu.make_async_remote_copy(
            src_ref=gat.at[block, span],
            dst_ref=gat.at[block, span],
            send_sem=g_send.at[kk, kind],
            recv_sem=g_recv.at[kk, kind],
            device_id={"ch": there},
            device_id_type=MESH,
        )

    sent = []
    stores = []

    def push(copy):
        copy.start()
        sent.append(copy)

    def begin(kk):
        at, size = starts[kk], sizes[kk]
        side, inside = at // wing, at % wing
        if inside == 0:
            take(y_sem.at[side, 1], recv_y.at[side, others])
        conv = recv_y[side, :, :, inside : inside + size].astype(F32).reshape(chans, size).T
        gated = outer[full[kk]] * (conv + direct[full[kk]])
        gat[place, full[kk]] = gated.astype(BF16)
        push(hop(kk, 0, place, full, right))
        push(hop(kk, 1, place, full, left))
        push(hop(kk, 2, place, full, base + f_place))

    def times(kk, block, side):
        return jnp.dot(gat[block, full[kk]], wide[block, side], preferred_element_type=F32)

    def near(kk, side):
        return times(kk, place, side) + times(kk, l_place, side) + times(kk, r_place, side)

    def share_out(kk):
        return pltpu.make_async_remote_copy(
            src_ref=give.at[full[kk]],
            dst_ref=gain.at[full[kk]],
            send_sem=p_sem.at[0, kk],
            recv_sem=p_sem.at[1, kk],
            device_id={"ch": across},
            device_id_type=MESH,
        )

    def combine(kk):
        hop(kk, 0, l_place, full, left).wait_recv()
        hop(kk, 1, r_place, full, right).wait_recv()
        theirs = near(kk, 1)
        hop(kk, 2, f_place, full, left).wait_recv()
        give[full[kk]] = (theirs + times(kk, f_place, 1)).astype(BF16)
        push(share_out(kk))
        acc[full[kk]] = near(kk, 0) + times(kk, f_place, 0)
        keep = pltpu.make_async_copy(acc.at[full[kk]], own_out.at[full[kk]], out_sem.at[kk])
        keep.start()
        stores.append(keep)

    for kk in range(last + 1):
        begin(kk)
    loads[5].wait()
    loads[6].wait()
    take(f_sem.at[1], lent)
    for kk in range(last + 1):
        combine(kk)
    for kk in range(last + 1):
        share_out(kk).wait_recv()

    edge.wait_send()
    take(h_sem.at[0], send_h.at[others])
    take(x_sem.at[0], send_x.at[others])
    for side in range(HALVES):
        take(y_sem.at[side, 0], recv_y.at[side, others])
    take(w_sem.at[0], lent)
    take(f_sem.at[0], lent)
    for copy in sent:
        copy.wait_send()
    for store in stores:
        store.wait()


def local(streams, short_taps, filters, skip_gain, out_weight, *, table):
    n_ctx, n_ch = lax.axis_size("ctx"), lax.axis_size("ch")
    seg, _, chans = streams.shape
    share = chans // n_ctx
    cols = out_weight.shape[1] // n_ch
    tiles = seg // LANES
    slabs = pltpu.VMEM((n_ctx, share, seg), BF16)
    wing = seg // HALVES
    parts = pltpu.VMEM((seg, cols), BF16)
    chunks = len(SPLITS)
    dma = pltpu.SemaphoreType.DMA
    own, gained = pl.pallas_call(
        functools.partial(operator_kernel, n_ctx, n_ch),
        out_shape=[
            jax.ShapeDtypeStruct((seg, cols), F32),
            jax.ShapeDtypeStruct((seg, cols), BF16),
        ],
        in_specs=[pl.BlockSpec(memory_space=pl.ANY)] * 6,
        out_specs=[pl.BlockSpec(memory_space=pl.ANY)] * 2,
        scratch_shapes=[
            pltpu.VMEM((3, seg, chans), BF16),
            pltpu.VMEM(short_taps.shape, F32),
            pltpu.VMEM((seg, chans), BF16),
            pltpu.VMEM((1, chans), F32),
            pltpu.VMEM((seg, 2 * seg), BF16),
            pltpu.VMEM((RING, 2, chans, cols), BF16),
            pltpu.VMEM((3, seg + 8, chans), F32),
            pltpu.VMEM((3, EDGE, chans), BF16),
            slabs,
            slabs,
            slabs,
            slabs,
            pltpu.VMEM((HALVES, 2, n_ctx // 2, share, wing), BF16),
            pltpu.VMEM((HALVES, n_ctx, share, wing), BF16),
            pltpu.VMEM((3, tiles, n_ctx, share, LANES), F32),
            pltpu.VMEM((3, tiles, n_ctx + LEAD, share, LANES), F32),
            pltpu.VMEM((2, n_ctx // 2 * share, 2 * seg), BF16),
            pltpu.VMEM((seg, chans), F32),
            pltpu.VMEM((seg, chans), F32),
            pltpu.VMEM((RING, seg, chans), BF16),
            parts,
            pltpu.VMEM((seg, cols), F32),
            dma((7,)),
            dma((2,)),
            dma((2,)),
            dma((2,)),
            dma((HALVES, 2)),
            dma((2,)),
            dma((2,)),
            dma((chunks, 4)),
            dma((chunks, 4)),
            dma((2, chunks)),
            dma((chunks,)),
        ],
        compiler_params=pltpu.CompilerParams(
            collective_id=0, has_side_effects=True, vmem_limit_bytes=67043328
        ),
        name="hyena_operator",
    )(
        jnp.transpose(streams, (1, 0, 2)),
        short_taps,
        filters,
        skip_gain[None],
        table,
        out_weight,
    )
    return (own + gained.astype(F32)).astype(BF16)


def solution(mesh):
    seg = 16384 // mesh.shape["ctx"]
    return jax.shard_map(
        functools.partial(local, table=half_table(2 * seg)),
        mesh=mesh,
        in_specs=(
            P("ctx", None, "ch"),
            P(None, None, "ch"),
            P("ctx", "ch"),
            P("ch"),
            P("ch", None),
        ),
        out_specs=P("ctx", "ch"),
        check_vma=False,
    )
```
